32 devices in a mesh: grp: 2 (over y), ccd: 4 (over z), row: 2 (over x), amp: 2 (over core).
Axes of the slice: x: 2, y: 2, z: 4, core: 2. Of those that a mesh axis runs over, the one named last changes fastest.
Arguments:
- science: float32 [8, 512, 1024], P(('grp', 'ccd'), 'row', 'amp'), parts along dimension 0, may hold values from -6 to 6
- template: bfloat16 [8, 2, 2, 8, 32, 512], P(('grp', 'ccd'), 'row', 'amp'), parts along dimension 0, may hold values from -6 to 6
- owners: int32 [8, 2, 2, 8, 1], P(('grp', 'ccd'), 'row', 'amp'), parts along dimension 0, may hold values from 0 to 3; in each aligned block of 8 rows (0 to 7, 8 to 15, ..., all dimensions but the last counted through in order) at most 2 rows name the same one
- patch_strip: int32 [8, 2, 2, 8], P(('grp', 'ccd'), 'row', 'amp'), parts along dimension 0, may hold values from 0 to 7
- shifts: int32 [8, 2, 2, 2, 8], P(('grp', 'ccd'), 'row', 'amp'), parts along dimension 0, may hold values from -3 to 3
- fractions: float32 [8, 2, 2, 2, 8], P(('grp', 'ccd'), 'row', 'amp'), parts along dimension 0, may hold values from 0.05 to 0.95
- coefs: float32 [8, 3, 9], P(('grp', 'ccd')), parts along dimension 0, may hold values from -3 to 3
Outputs:
- difference: float32 [8, 512, 1024], P(('grp', 'ccd'), 'row', 'amp'), parts along dimension 0
- stack: float32 [8, 2, 2, 8, 32, 512], P(('grp', 'ccd'), 'row', 'amp'), parts along dimension 0
The draws below stay inside these ranges and needn't reach their ends.
There are 2 independent parts, one for each index of `grp`. The reference program is written for one: setup_inputs(seed, part) draws one part's arguments, and reference() takes and returns one part's arrays. A program takes and returns all parts, laid end to end along the dimension named above; each array names one. Nothing has to cross between parts.
Inputs may be any that keep to these rules, and one draw needn't show every extreme that they name: Among the 8 strips of one device's block no owner is named more than 2 times, and some block names one owner exactly 2 times in every draw; owners lie in the same row band and column half as the block.
All inputs are finite; a program needn't handle non-finite values.
Results may differ from the reference program's by a relative error of at most 0.0057.
Values may be sent and summed in bfloat16 or wider, within the bound.
A program may use at most 64 MiB of HBM per device.

```python
import math
import jax
import jax.numpy as jnp
import numpy as np
from jax import lax

BAND = 256
HALF = 512
STRIP_ROWS = 32
RADIUS = 9
CCDS = 4
BANDS = 2
HALVES = 2
STRIPS = 8
CAP = 2
IMG_ROWS = 512
IMG_COLS = 1024


def with_ends(array, key, smallest, largest):
    index_at = [jax.random.randint(jax.random.fold_in(key, axis), (), 0, length) for axis, length in enumerate(array.shape)]
    widest = array.shape.index(max(array.shape))
    neighbour = index_at[:widest] + [(index_at[widest] + 1) % array.shape[widest]] + index_at[widest + 1:]
    return array.at[tuple(index_at)].set(smallest).at[tuple(neighbour)].set(largest)


def levels(key, dims, shards, smallest, largest):
    gain = 1.0
    for axis_at, shards_of in shards:
        steps = jax.random.uniform(jax.random.fold_in(jax.random.fold_in(key, 6), axis_at), (shards_of,), jnp.float32, smallest / len(shards), largest / len(shards))
        gain = gain * jnp.repeat(jnp.exp(steps), dims[axis_at] // shards_of).reshape((-1,) + (1,) * (len(dims) - 1 - axis_at))
    return gain


def shared_out(own_key, own, number, rows, number_of, top, limit, lean):
    ranking = jax.random.permutation(own_key, number_of)
    packed, common = portions_of(number_of, rows * top, limit, lean, True), portions_of(number_of, rows * top, limit, lean, False)
    places = jnp.arange(number_of)

    def named(sizes, turn):
        used = int((sizes > 0).sum())
        fixed = max(1, used // 4)
        passed = fixed + (places - fixed + turn * (used - fixed)) % max(1, number_of - fixed)
        return jnp.zeros((number_of,), jnp.int32).at[ranking[jnp.where(places < fixed, places, passed)]].set(jnp.asarray(sizes, jnp.int32))

    sizes = jnp.where(number % 4 == 0, named(packed, number // 4), named(common, number - number // 4 - 1))
    mixed = jax.random.permutation(jax.random.fold_in(own, 3), number_of)
    donor, receiver = mixed[0:number_of // 2 * 2:2], mixed[1:number_of // 2 * 2:2]
    room = jnp.minimum(sizes[donor] - 1, limit - sizes[receiver]) // 2
    room = jnp.where((donor == ranking[0]) | (receiver == ranking[0]) | (sizes[receiver] == 0), 0, jnp.maximum(room, 0))
    passed = jax.random.randint(jax.random.fold_in(own, 4), (number_of // 2,), 0, 1 << 20) % (room + 1)
    sizes = sizes.at[donor].add(-passed).at[receiver].add(passed)
    members = jnp.searchsorted(jnp.cumsum(sizes), jnp.arange(rows * top), side="right").astype(jnp.int32)
    listing = members.reshape(top, rows).T
    listing = listing[jax.random.permutation(jax.random.fold_in(own, 1), rows)]
    turn = jax.random.randint(jax.random.fold_in(own, 2), (rows, 1), 0, top)
    return jnp.take_along_axis(listing, (jnp.arange(top)[None, :] + turn) % top, axis=1)


def portions_of(count, total, reach, skew, full):
    weights = [(1 << 20) // math.isqrt(rank ** skew) + 1 for rank in range(1, count + 1)]
    largest = reach if full else min(reach, max(-(-total // count), total * weights[0] // sum(weights)))
    least = 1 if total - largest >= count - 1 else 0
    given, spare = [largest] + [least] * (count - 1), total - largest - least * (count - 1)
    while spare > 0:
        movable = [i for i in range(1, count) if given[i] < largest] or [i for i in range(1, count) if given[i] < reach]
        pool, left = sum([weights[i] for i in movable]), spare
        for i in movable:
            addition = min(reach - given[i], max(1, left * weights[i] // pool), spare)
            given[i] = given[i] + addition
            spare = spare - addition
    return np.array(given)


def centred(own_key, extent, scale, bound, split=(), held_as=jnp.bfloat16):
    entries = scale * jax.random.normal(own_key, extent, jnp.float32)
    if split:
        entries = entries * levels(own_key, extent, split, -0.22, 0.18)
    return jnp.clip(entries, -bound, bound).astype(held_as)


def setup_inputs(seed: int = 0, part: int = 0) -> dict:
    keys = jax.random.split(jax.random.key(seed), 8)
    own_keys = jax.random.split(jax.random.fold_in(keys[7], part), 8)
    science = centred(own_keys[0], (CCDS, IMG_ROWS, IMG_COLS), 1.0, 6.0, ((0, 4), (1, 2), (2, 2)), jnp.float32)
    template = centred(own_keys[1], (CCDS, BANDS, HALVES, STRIPS, STRIP_ROWS, HALF), 1.0, 6.0, ((0, 4), (1, 2), (2, 2)))
    owners_keys = jax.random.split(jax.random.fold_in(own_keys[2], 1), CCDS * BANDS * HALVES * STRIPS // STRIPS)
    owners_turns = jax.random.permutation(jax.random.fold_in(own_keys[2], 3), CCDS * BANDS * HALVES * STRIPS // STRIPS)
    owners = jax.vmap(lambda own, number: shared_out(jax.random.fold_in(own_keys[2], 2), own, number, STRIPS, CCDS, 1, CAP, 2))(owners_keys, owners_turns).reshape((CCDS, BANDS, HALVES, STRIPS, 1))
    patch_strip = with_ends(jax.random.randint(own_keys[3], (CCDS, BANDS, HALVES, STRIPS), 0, STRIPS), jax.random.fold_in(own_keys[3], 1), 0, STRIPS - 1).astype(jnp.int32)
    shifts = with_ends(jax.random.randint(own_keys[4], (CCDS, BANDS, HALVES, 2, STRIPS), -3, 4), jax.random.fold_in(own_keys[4], 1), -3, 3).astype(jnp.int32)
    fractions = jnp.clip(0.05 + 0.9 * jax.random.uniform(own_keys[5], (CCDS, BANDS, HALVES, 2, STRIPS), jnp.float32) ** levels(own_keys[5], (CCDS, BANDS, HALVES, 2, STRIPS), ((0, 4), (1, 2), (2, 2)), -0.2, 0.2), 0.05, 0.95)
    coefs = centred(own_keys[6], (CCDS, 3, 9), 0.5, 3.0, ((0, 4),), jnp.float32)
    return {"science": science, "template": template, "owners": owners, "patch_strip": patch_strip, "shifts": shifts, "fractions": fractions, "coefs": coefs}


tap_margin = 6


def lanczos_taps(fraction):
    offsets = jnp.arange(-2, 4).astype(jnp.float32)
    spread = offsets[None, :] - fraction[:, None]
    return (jnp.sinc(spread) * jnp.sinc(spread / 3.0)).astype(jnp.bfloat16)


def kernel_table():
    support = jnp.arange(-RADIUS, RADIUS + 1).astype(jnp.float32)
    narrow = jnp.exp(-support * support / 4.5)
    slope = support * jnp.exp(-support * support / 12.5)
    broad = jnp.exp(-support * support / 40.5)
    return jnp.stack([narrow / jnp.sum(narrow), slope / jnp.sum(jnp.abs(slope)), broad / jnp.sum(broad)]).astype(jnp.bfloat16)


def strip_operator(taps, shift, strip_rows):
    out_rows = jnp.arange(strip_rows).astype(jnp.int32)[None, :, None]
    src_rows = jnp.arange(strip_rows).astype(jnp.int32)[None, None, :]
    offset = src_rows - out_rows - shift.astype(jnp.int32)[:, None, None]
    table = jnp.zeros(offset.shape, jnp.bfloat16)
    for which in range(6):
        table = jnp.where(offset == which - 2, taps[:, which][:, None, None], table)
    return table


def shift_columns(values, taps, starts, width):
    def one_strip(block, tap_row, start_row):
        total = jnp.zeros((block.shape[0], width), jnp.float32)
        for which in range(6):
            moved = lax.dynamic_slice_in_dim(block, start_row[which], width, 1)
            total = total + tap_row[which].astype(jnp.float32) * moved.astype(jnp.float32)
        return total
    return jax.vmap(one_strip)(values, taps, starts)


def tap_steps():
    return (jnp.arange(6) - 2).astype(jnp.int32)


def forward_warp(block, shift_pair, fraction_pair):
    strip_rows = block.shape[1]
    width = block.shape[2]
    row_taps = lanczos_taps(fraction_pair[0])
    col_taps = lanczos_taps(fraction_pair[1])
    operator = strip_operator(row_taps, shift_pair[0], strip_rows)
    rows_done = jnp.einsum("qik,qkz->qiz", operator.astype(jnp.float32), block.astype(jnp.float32)).astype(jnp.bfloat16)
    starts = (tap_margin + shift_pair[1].astype(jnp.int32)[:, None] + tap_steps()[None, :]).astype(jnp.int32)
    padded = jnp.pad(rows_done, ((0, 0), (0, 0), (tap_margin, tap_margin)))
    return shift_columns(padded, col_taps, starts, width).astype(jnp.bfloat16)


def backward_warp(block, shift_pair, fraction_pair):
    strip_rows = block.shape[1]
    width = block.shape[2]
    row_taps = lanczos_taps(fraction_pair[0])
    col_taps = lanczos_taps(fraction_pair[1])
    operator = strip_operator(row_taps, shift_pair[0], strip_rows)
    starts = (tap_margin - shift_pair[1].astype(jnp.int32)[:, None] - tap_steps()[None, :]).astype(jnp.int32)
    padded = jnp.pad(block, ((0, 0), (0, 0), (tap_margin, tap_margin)))
    columns_back = shift_columns(padded, col_taps, starts, width).astype(jnp.bfloat16)
    return jnp.einsum("qik,qiz->qkz", operator.astype(jnp.float32), columns_back.astype(jnp.float32))


def reference(science, template, owners, patch_strip, shifts, fractions, coefs):
    kernels = kernel_table()
    owner_all = owners[..., 0]
    band_index = jnp.arange(BANDS).astype(jnp.int32)[None, :, None, None]
    half_index = jnp.arange(HALVES).astype(jnp.int32)[None, None, :, None]
    chosen_all = template[owner_all, band_index, half_index, patch_strip]
    row_place = (jnp.arange(IMG_ROWS) + 0.5) / IMG_ROWS * 2.0 - 1.0
    col_place = (jnp.arange(IMG_COLS) + 0.5) / IMG_COLS * 2.0 - 1.0
    blocks = BANDS * HALVES
    width = 2 * RADIUS + 1

    def one_ccd(inputs):
        chosen, image_science, shift_ccd, fraction_ccd, coef_ccd = inputs
        chosen_flat = chosen.reshape(blocks, STRIPS, STRIP_ROWS, HALF)
        shift_flat = shift_ccd.reshape(blocks, 2, STRIPS)
        fraction_flat = fraction_ccd.reshape(blocks, 2, STRIPS)
        warped = jax.vmap(forward_warp)(chosen_flat, shift_flat, fraction_flat)
        image = warped.reshape(BANDS, HALVES, BAND, HALF).transpose(0, 2, 1, 3).reshape(IMG_ROWS, IMG_COLS)
        padded = jnp.pad(image, RADIUS)
        model = jnp.zeros((IMG_ROWS, IMG_COLS), jnp.float32)
        for first in range(3):
            across = jnp.zeros((IMG_ROWS, IMG_COLS + 2 * RADIUS), jnp.float32)
            for offset in range(width):
                across = across + kernels[first, offset].astype(jnp.float32) * padded[offset:offset + IMG_ROWS, :].astype(jnp.float32)
            across = across.astype(jnp.bfloat16)
            for second in range(3):
                term = jnp.zeros((IMG_ROWS, IMG_COLS), jnp.float32)
                for offset in range(width):
                    term = term + kernels[second, offset].astype(jnp.float32) * across[:, offset:offset + IMG_COLS].astype(jnp.float32)
                basis = first * 3 + second
                weight = coef_ccd[0, basis] + coef_ccd[1, basis] * col_place[None, :] + coef_ccd[2, basis] * row_place[:, None]
                model = model + weight * term
        difference = image_science - model
        lowered = difference.astype(jnp.bfloat16).reshape(BANDS, BAND, HALVES, HALF).transpose(0, 2, 1, 3)
        lowered = lowered.reshape(blocks, STRIPS, STRIP_ROWS, HALF)
        contribution = jax.vmap(backward_warp)(lowered, shift_flat, fraction_flat)
        return difference, contribution.reshape(BANDS, HALVES, STRIPS, STRIP_ROWS, HALF)

    differences, contributions = lax.map(one_ccd, (chosen_all, science, shifts, fractions, coefs))
    stack = jnp.zeros(template.shape, jnp.float32).at[owner_all, band_index, half_index, patch_strip].add(contributions)
    return differences, stack
```

```python
import functools

import jax
import jax.numpy as jnp
import ml_dtypes
import numpy as np
from jax import lax
from jax.experimental import pallas as pl
from jax.experimental.pallas import tpu as pltpu
from jax.sharding import PartitionSpec as P

RADIUS = 9
EDGE = 16
LANES = 128
TILE = 256
MESH = pl.DeviceIdType.MESH
F32 = jnp.float32
BF16 = jnp.bfloat16


def kernel_table():
    support = np.arange(-RADIUS, RADIUS + 1).astype(np.float32)
    narrow = np.exp(-support * support / np.float32(4.5))
    slope = support * np.exp(-support * support / np.float32(12.5))
    broad = np.exp(-support * support / np.float32(40.5))
    table = np.stack(
        [narrow / np.sum(narrow), slope / np.sum(np.abs(slope)), broad / np.sum(broad)]
    )
    return table.astype(ml_dtypes.bfloat16)


def toeplitz(kernel, out_at, in_at):
    offset = in_at[None, :] - out_at[:, None] + RADIUS
    inside = (offset >= 0) & (offset <= 2 * RADIUS)
    return np.where(inside, kernel[np.clip(offset, 0, 2 * RADIUS)], np.zeros((), kernel.dtype))


def conv_constants(rows, window):
    table = kernel_table()
    at = np.arange(rows)
    main = np.concatenate([toeplitz(k, at, at) for k in table], axis=0)
    top = np.stack([toeplitz(k, np.arange(EDGE), np.arange(-EDGE, 0)) for k in table])
    bottom = np.stack(
        [toeplitz(k, np.arange(-EDGE, 0), np.arange(EDGE)) for k in table]
    )
    source = np.arange(-EDGE, TILE + EDGE)
    cols = np.stack([toeplitz(k, np.arange(TILE), source).T for k in table])
    return main, np.stack([top, bottom]), cols


def sinc(value):
    angle = np.float32(np.pi) * value
    return jnp.sin(angle) / angle


def taps_of(offset):
    value = sinc(offset) * sinc(offset / 3.0)
    return value.astype(BF16).astype(F32)


def kernel(
    sci_hbm, tmpl_hbm, own_hbm, pat_hbm, shf_hbm, frc_hbm, cof_hbm, kmain_hbm, kedge_hbm, kcol_hbm,
    diff_hbm, stack_hbm,
    sci, tmpl, own, pat, shf, frc, cof, kmain, kedge, kcol,
    req_out, req_in, meta_out, meta_in, send_buf, fetch, warp_op, taps_fwd, taps_bwd, slot_img,
    img, top_halo, bottom_halo, edge_acc, across, col_op, acc, diff, low, back_out, back_in, back_op, stack,
    load_sem, store_sem, req_send, req_recv, meta_send, meta_recv, tmpl_send, tmpl_recv,
    halo_send, halo_recv, back_send, back_recv,
    *, capacity,
):
    n = lax.axis_size("ccd")
    rows_n = lax.axis_size("row")
    cols_n = lax.axis_size("amp")
    me = lax.axis_index("ccd")
    my_row = lax.axis_index("row")
    my_col = lax.axis_index("amp")
    strips, srows, width = tmpl.shape
    band = strips * srows
    span = capacity * srows
    slots = n * capacity

    def peer(d):
        return {"ccd": lax.rem(me + d, n)}

    def back_peer(d):
        return {"ccd": lax.rem(me + n - d, n)}

    loads = [
        pltpu.make_async_copy(src, dst, load_sem.at[i])
        for i, (src, dst) in enumerate(
            [(own_hbm, own), (pat_hbm, pat), (shf_hbm, shf), (frc_hbm, frc), (cof_hbm, cof),
             (tmpl_hbm, tmpl), (kmain_hbm, kmain), (kedge_hbm, kedge), (kcol_hbm, kcol), (sci_hbm, sci)]
        )
    ]
    for load in loads:
        load.start()

    steps = [(-1, 0), (1, 0), (0, -1), (0, 1), (-1, -1), (-1, 1), (1, -1), (1, 1)]

    def has(step):
        ok_row = (my_row + step[0] >= 0) & (my_row + step[0] < rows_n)
        ok_col = (my_col + step[1] >= 0) & (my_col + step[1] < cols_n)
        return ok_row & ok_col

    def neighbour(step):
        return {"row": my_row + step[0], "amp": my_col + step[1]}

    barrier = pltpu.get_barrier_semaphore()
    for d in range(1, n):
        pl.semaphore_signal(barrier, inc=1, device_id=peer(d), device_id_type=MESH)
    for step in steps:
        @pl.when(has(step))
        def _():
            pl.semaphore_signal(barrier, inc=1, device_id=neighbour(step), device_id_type=MESH)

    for i in range(5):
        loads[i].wait()
    owner = [own[0, q] for q in range(strips)]
    slot_of = []
    for q in range(strips):
        rank = jnp.int32(0)
        for e in range(q):
            rank = rank + jnp.where(owner[e] == owner[q], 1, 0)
        away = owner[q] - me
        away = jnp.where(away < 0, away + n, away)
        slot_of.append(jnp.minimum(away * capacity + rank, slots - 1))
    strip_of = []
    wanted = []
    for s in range(slots):
        q_at = jnp.int32(-1)
        for q in range(strips):
            q_at = jnp.where(slot_of[q] == s, q, q_at)
        q_in = jnp.maximum(q_at, 0)
        strip_of.append(q_in)
        wanted.append(jnp.where(q_at < 0, -1, pat[0, q_in]))
    for d in range(1, n):
        for r in range(capacity):
            req_out[d, r] = wanted[d * capacity + r]

    around = jnp.int32(n - 1)
    for step in steps:
        around = around + jnp.where(has(step), 1, 0)
    pl.semaphore_wait(barrier, around)

    def request(d):
        return pltpu.make_async_remote_copy(
            src_ref=req_out.at[d], dst_ref=req_in.at[d], send_sem=req_send.at[d], recv_sem=req_recv.at[d],
            device_id=peer(d), device_id_type=MESH)

    for d in range(1, n):
        request(d).start()

    loads[5].wait()
    for r in range(capacity):
        fetch[0, r * srows:(r + 1) * srows, :] = tmpl[jnp.maximum(wanted[r], 0)]

    def reply(d):
        return pltpu.make_async_remote_copy(
            src_ref=send_buf.at[d], dst_ref=fetch.at[d], send_sem=tmpl_send.at[d], recv_sem=tmpl_recv.at[d],
            device_id=back_peer(d), device_id_type=MESH)

    for d in range(1, n):
        request(d).wait_recv()
        for r in range(capacity):
            send_buf[d, r * srows:(r + 1) * srows, :] = tmpl[jnp.maximum(req_in[d, r], 0)]
        reply(d).start()

    lane = lax.broadcasted_iota(jnp.int32, (8, LANES), 1)
    sub = lax.broadcasted_iota(jnp.int32, (8, LANES), 0)
    tap = (sub - 2).astype(F32)

    def meta(d):
        return pltpu.make_async_remote_copy(
            src_ref=meta_out.at[d], dst_ref=meta_in.at[d], send_sem=meta_send.at[d], recv_sem=meta_recv.at[d],
            device_id=peer(d), device_id_type=MESH)

    for d in range(n):
        frac = jnp.full((8, LANES), 0.5, F32)
        shift = jnp.zeros((8, LANES), F32)
        which = jnp.full((8, LANES), -1.0, F32)
        for r in range(capacity):
            s = d * capacity + r
            mine = (lane >= r * srows) & (lane < (r + 1) * srows)
            frac = jnp.where(mine, frc[0, strip_of[s]], frac)
            shift = jnp.where(mine, shf[0, strip_of[s]].astype(F32), shift)
            which = jnp.where(mine, wanted[s].astype(F32), which)
        taps = taps_of(tap - frac)
        meta_out[d] = jnp.where(sub == 6, shift, jnp.where(sub == 7, which, taps))
        if d:
            meta(d).start()

    row_at = lax.broadcasted_iota(jnp.int32, (srows, LANES), 0)
    lane_at = lax.broadcasted_iota(jnp.int32, (srows, LANES), 1)
    lane_in = lax.rem(lane_at, srows)

    def place(table, offset):
        total = jnp.zeros((srows, LANES), F32)
        for t in range(6):
            total = jnp.where(offset == t - 2, table[t:t + 1, :], total)
        return total

    for d in range(n):
        table = meta_out[d]
        shift = table[6:7, :].astype(jnp.int32)
        operator = place(table, lane_in - row_at - shift)
        for r in range(capacity):
            mine = (lane_at >= r * srows) & (lane_at < (r + 1) * srows)
            warp_op[d, r * srows:(r + 1) * srows, :] = jnp.where(mine, operator, 0.0).astype(BF16)

    col_at = lax.broadcasted_iota(jnp.int32, (8, width), 1)
    tap_at = lax.broadcasted_iota(jnp.int32, (8, width), 0) - 2
    for s in range(slots):
        taps = taps_of(tap - frc[1, strip_of[s]])
        wide = jnp.concatenate([taps] * (width // LANES), axis=1)
        moved = tap_at + shf[1, strip_of[s]]
        ahead, behind = col_at + moved, col_at - moved
        taps_fwd[s] = jnp.where((ahead >= 0) & (ahead < width), wide, 0.0)
        taps_bwd[s] = jnp.where((behind >= 0) & (behind < width), wide, 0.0)

    for i in range(6, 9):
        loads[i].wait()
    halves = width // TILE
    window = 2 * TILE
    first = LANES - EDGE
    last = LANES + TILE + EDGE
    place_x = lax.broadcasted_iota(jnp.int32, (1, TILE), 1).astype(F32) + (my_col * width).astype(F32)
    for h in range(halves):
        for a in range(3):
            col_op[h, a * window:a * window + first, :] = jnp.zeros((first, 2 * TILE), BF16)
            col_op[h, a * window + last:(a + 1) * window, :] = jnp.zeros((window - last, 2 * TILE), BF16)
    chunk = 48
    for a in range(3):
        @pl.loop(0, (last - first) // chunk)
        def _(i):
            at = pl.ds(pl.multiple_of(i * chunk, 16), chunk)
            base = [kcol[b, at, :].astype(F32) for b in range(3)]
            fold = [
                cof[j, 3 * a] * base[0] + cof[j, 3 * a + 1] * base[1] + cof[j, 3 * a + 2] * base[2]
                for j in range(3)
            ]
            to = pl.ds(pl.multiple_of(a * window + first + i * chunk, 16), chunk)
            for h in range(halves):
                px = (place_x + (h * TILE + 0.5)) / (width * cols_n) * 2.0 - 1.0
                col_op[h, to, 0:TILE] = (fold[0] + px * fold[1]).astype(BF16)
                col_op[h, to, TILE:] = fold[2].astype(BF16)

    for d in range(n):
        if d:
            meta(d).wait_recv()
        table = meta_in[d] if d else meta_out[0]
        shift = table[6:7, :].astype(jnp.int32)
        which = table[7:8, :].astype(jnp.int32)
        operator = place(table, row_at - lane_in - shift)
        for p in range(strips):
            back_op[d, p * srows:(p + 1) * srows, :] = jnp.where(which == p, operator, 0.0).astype(BF16)

    @pl.when(my_row == 0)
    def _():
        top_halo[...] = jnp.zeros_like(top_halo)

    @pl.when(my_row == rows_n - 1)
    def _():
        bottom_halo[...] = jnp.zeros_like(bottom_halo)

    right = LANES + width

    @pl.when(my_col == 0)
    def _():
        img[:, 0:LANES] = jnp.zeros((band, LANES), BF16)
        top_halo[:, 0:LANES] = jnp.zeros((EDGE, LANES), BF16)
        bottom_halo[:, 0:LANES] = jnp.zeros((EDGE, LANES), BF16)

    @pl.when(my_col == cols_n - 1)
    def _():
        img[:, right:] = jnp.zeros((band, LANES), BF16)
        top_halo[:, right:] = jnp.zeros((EDGE, LANES), BF16)
        bottom_halo[:, right:] = jnp.zeros((EDGE, LANES), BF16)

    for d in range(n):
        if d:
            reply(d).wait_recv()
        rows_done = jnp.dot(warp_op[d, :, :span], fetch[d], preferred_element_type=F32).astype(BF16)
        for r in range(capacity):
            s = d * capacity + r
            value = rows_done[r * srows:(r + 1) * srows, :]
            move = shf[1, strip_of[s]]
            total = jnp.zeros((srows, width), F32)
            for t in range(6):
                moved = pltpu.roll(value, width - (move + (t - 2)), 1).astype(F32)
                total = total + taps_fwd[s, t:t + 1, :] * moved
            slot_img[s] = total.astype(BF16)
    for q in range(strips):
        img[q * srows:(q + 1) * srows, LANES:right] = slot_img[slot_of[q]]

    def halo(i):
        step = steps[i]
        src = dst = None
        if step[1] == 0:
            cols_src = cols_dst = pl.ds(LANES, width)
        elif step[1] < 0:
            cols_src, cols_dst = pl.ds(LANES, LANES), pl.ds(right, LANES)
        else:
            cols_src, cols_dst = pl.ds(right - LANES, LANES), pl.ds(0, LANES)
        if step[0] == 0:
            src, dst = img.at[:, cols_src], img.at[:, cols_dst]
        elif step[0] < 0:
            src, dst = img.at[pl.ds(0, EDGE), cols_src], bottom_halo.at[:, cols_dst]
        else:
            src, dst = img.at[pl.ds(band - EDGE, EDGE), cols_src], top_halo.at[:, cols_dst]
        return pltpu.make_async_remote_copy(
            src_ref=src, dst_ref=dst, send_sem=halo_send.at[i], recv_sem=halo_recv.at[i],
            device_id=neighbour(step), device_id_type=MESH)

    for i, step in enumerate(steps):
        @pl.when(has(step))
        def _(i=i):
            halo(i).start()

    def put(a, row, count, col, value):
        value = value.astype(BF16)
        for h in range(halves):
            begin, end = h * TILE, h * TILE + window
            lo, hi = max(begin, col), min(end, col + value.shape[1])
            if lo < hi:
                across[h, row:row + count, a * window + lo - begin:a * window + hi - begin] = value[:, lo - col:hi - col]

    for c in range(width // TILE):
        col = LANES + c * TILE
        for a in range(3):
            part = jnp.dot(kmain[a * band:(a + 1) * band, :], img[:, col:col + TILE], preferred_element_type=F32)
            put(a, EDGE, band - 2 * EDGE, col, part[EDGE:band - EDGE, :])
            edge_acc[a, 0:EDGE, col:col + TILE] = part[0:EDGE, :]
            edge_acc[a, EDGE:, col:col + TILE] = part[band - EDGE:, :]

    def received(step):
        return (-step[0], -step[1])

    for i, step in enumerate(steps):
        @pl.when(has(received(step)))
        def _(i=i):
            halo(i).wait_recv()

    for col in (0, right):
        for a in range(3):
            part = jnp.dot(kmain[a * band:(a + 1) * band, :], img[:, col:col + LANES], preferred_element_type=F32)
            put(a, EDGE, band - 2 * EDGE, col, part[EDGE:band - EDGE, :])
            edge_acc[a, 0:EDGE, col:col + LANES] = part[0:EDGE, :]
            edge_acc[a, EDGE:, col:col + LANES] = part[band - EDGE:, :]
    for a in range(3):
        upper = edge_acc[a, 0:EDGE, :] + jnp.dot(kedge[0, a], top_halo[...], preferred_element_type=F32)
        lower = edge_acc[a, EDGE:, :] + jnp.dot(kedge[1, a], bottom_halo[...], preferred_element_type=F32)
        put(a, 0, EDGE, 0, upper)
        put(a, band - EDGE, EDGE, 0, lower)

    loads[9].wait()
    place_y = lax.broadcasted_iota(jnp.int32, (band, LANES), 0) + my_row * band
    py = (place_y.astype(F32) + 0.5) / (band * rows_n) * 2.0 - 1.0
    py = jnp.concatenate([py] * (TILE // LANES), axis=1)
    for h in range(halves):
        acc[...] = jnp.dot(across[h], col_op[h], preferred_element_type=F32)
        at = slice(h * TILE, (h + 1) * TILE)
        value = sci[:, at] - (acc[:, 0:TILE] + py * acc[:, TILE:])
        diff[:, at] = value
        for q in range(strips):
            low[q, :, at] = value[q * srows:(q + 1) * srows, :].astype(BF16)
    keep = pltpu.make_async_copy(diff, diff_hbm, store_sem.at[0])
    keep.start()

    def give(d):
        return pltpu.make_async_remote_copy(
            src_ref=back_out.at[d], dst_ref=back_in.at[d], send_sem=back_send.at[d], recv_sem=back_recv.at[d],
            device_id=peer(d), device_id_type=MESH)

    for d in list(range(1, n)) + [0]:
        for r in range(capacity):
            s = d * capacity + r
            value = low[strip_of[s]]
            move = shf[1, strip_of[s]]
            total = jnp.zeros((srows, width), F32)
            for t in range(6):
                moved = pltpu.roll(value, width + (move + (t - 2)), 1).astype(F32)
                total = total + taps_bwd[s, t:t + 1, :] * moved
            back_out[d, r * srows:(r + 1) * srows, :] = total.astype(BF16)
        if d:
            give(d).start()

    stack[...] = jnp.dot(back_op[0, :, :span], back_out[0], preferred_element_type=F32)
    for d in range(1, n):
        give(d).wait_recv()
        stack[...] += jnp.dot(back_op[d, :, :span], back_in[d], preferred_element_type=F32)
    store = pltpu.make_async_copy(stack, stack_hbm, store_sem.at[1])
    store.start()

    for d in range(1, n):
        request(d).wait_send()
        reply(d).wait_send()
        meta(d).wait_send()
        give(d).wait_send()
    for i, step in enumerate(steps):
        @pl.when(has(step))
        def _(i=i):
            halo(i).wait_send()
    keep.wait()
    store.wait()


def body(science, template, owners, patch_strip, shifts, fractions, coefs):
    n = lax.axis_size("ccd")
    band, width = science.shape[1:]
    strips, srows = template.shape[3:5]
    capacity = max(2, strips // n)
    slots = n * capacity
    span = capacity * srows
    padded = width + 2 * LANES
    window = 2 * TILE
    halves = width // TILE
    kmain, kedge, kcol = conv_constants(band, window)
    any_spec = pl.BlockSpec(memory_space=pl.ANY)
    dma = pltpu.SemaphoreType.DMA
    scratch = [
        pltpu.VMEM((band, width), F32),
        pltpu.VMEM((strips, srows, width), BF16),
        pltpu.SMEM((1, strips), jnp.int32),
        pltpu.SMEM((1, strips), jnp.int32),
        pltpu.SMEM((2, strips), jnp.int32),
        pltpu.SMEM((2, strips), F32),
        pltpu.SMEM((3, 9), F32),
        pltpu.VMEM(kmain.shape, BF16),
        pltpu.VMEM(kedge.shape, BF16),
        pltpu.VMEM(kcol.shape, BF16),
        pltpu.SMEM((n, LANES), jnp.int32),
        pltpu.SMEM((n, LANES), jnp.int32),
        pltpu.VMEM((n, 8, LANES), F32),
        pltpu.VMEM((n, 8, LANES), F32),
        pltpu.VMEM((n, span, width), BF16),
        pltpu.VMEM((n, span, width), BF16),
        pltpu.VMEM((n, span, LANES), BF16),
        pltpu.VMEM((slots, 8, width), F32),
        pltpu.VMEM((slots, 8, width), F32),
        pltpu.VMEM((slots, srows, width), BF16),
        pltpu.VMEM((band, padded), BF16),
        pltpu.VMEM((EDGE, padded), BF16),
        pltpu.VMEM((EDGE, padded), BF16),
        pltpu.VMEM((3, 2 * EDGE, padded), F32),
        pltpu.VMEM((halves, band, 3 * window), BF16),
        pltpu.VMEM((halves, 3 * window, 2 * TILE), BF16),
        pltpu.VMEM((band, 2 * TILE), F32),
        pltpu.VMEM((band, width), F32),
        pltpu.VMEM((strips, srows, width), BF16),
        pltpu.VMEM((n, span, width), BF16),
        pltpu.VMEM((n, span, width), BF16),
        pltpu.VMEM((n, band, LANES), BF16),
        pltpu.VMEM((band, width), F32),
        dma((10,)),
        dma((2,)),
        dma((n,)), dma((n,)), dma((n,)), dma((n,)), dma((n,)), dma((n,)),
        dma((8,)), dma((8,)),
        dma((n,)), dma((n,)),
    ]
    difference, stack = pl.pallas_call(
        functools.partial(kernel, capacity=capacity),
        out_shape=(
            jax.ShapeDtypeStruct((band, width), F32),
            jax.ShapeDtypeStruct((band, width), F32),
        ),
        in_specs=[any_spec] * 10,
        out_specs=(any_spec, any_spec),
        scratch_shapes=scratch,
        compiler_params=pltpu.CompilerParams(
            collective_id=0, has_side_effects=True, vmem_limit_bytes=40 * 1024 * 1024
        ),
    )(
        science[0],
        template.reshape(strips, srows, width),
        owners.reshape(1, strips),
        patch_strip.reshape(1, strips),
        shifts.reshape(2, strips),
        fractions.reshape(2, strips),
        coefs[0],
        jnp.asarray(kmain),
        jnp.asarray(kedge),
        jnp.asarray(kcol),
    )
    return difference[None], stack.reshape(template.shape)


def solution(mesh):
    return jax.shard_map(
        body,
        mesh=mesh,
        in_specs=(
            P(("grp", "ccd"), "row", "amp"),
            P(("grp", "ccd"), "row", "amp", None, None, None),
            P(("grp", "ccd"), "row", "amp", None, None),
            P(("grp", "ccd"), "row", "amp", None),
            P(("grp", "ccd"), "row", "amp", None, None),
            P(("grp", "ccd"), "row", "amp", None, None),
            P(("grp", "ccd"), None, None),
        ),
        out_specs=(
            P(("grp", "ccd"), "row", "amp"),
            P(("grp", "ccd"), "row", "amp", None, None, None),
        ),
        check_vma=False,
    )
```

```python
import functools

import jax
import jax.numpy as jnp
import ml_dtypes
import numpy as np
from jax import lax
from jax.experimental import pallas as pl
from jax.experimental.pallas import tpu as pltpu
from jax.sharding import PartitionSpec as P

RADIUS = 9
EDGE = 16
LANES = 128
TILE = 256
MESH = pl.DeviceIdType.MESH
F32 = jnp.float32
BF16 = jnp.bfloat16


def kernel_table():
    support = np.arange(-RADIUS, RADIUS + 1).astype(np.float32)
    narrow = np.exp(-support * support / np.float32(4.5))
    slope = support * np.exp(-support * support / np.float32(12.5))
    broad = np.exp(-support * support / np.float32(40.5))
    table = np.stack(
        [narrow / np.sum(narrow), slope / np.sum(np.abs(slope)), broad / np.sum(broad)]
    )
    return table.astype(ml_dtypes.bfloat16)


def toeplitz(kernel, out_at, in_at):
    offset = in_at[None, :] - out_at[:, None] + RADIUS
    inside = (offset >= 0) & (offset <= 2 * RADIUS)
    return np.where(inside, kernel[np.clip(offset, 0, 2 * RADIUS)], np.zeros((), kernel.dtype))


def conv_constants(rows, window):
    table = kernel_table()
    at = np.arange(rows)
    main = np.concatenate([toeplitz(k, at, at) for k in table], axis=0)
    top = np.stack([toeplitz(k, np.arange(EDGE), np.arange(-EDGE, 0)) for k in table])
    bottom = np.stack(
        [toeplitz(k, np.arange(-EDGE, 0), np.arange(EDGE)) for k in table]
    )
    source = np.arange(-EDGE, TILE + EDGE)
    cols = np.stack([toeplitz(k, np.arange(TILE), source).T for k in table])
    return main, np.stack([top, bottom]), cols


def sinc(value):
    angle = np.float32(np.pi) * value
    return jnp.sin(angle) / angle


def taps_of(offset):
    value = sinc(offset) * sinc(offset / 3.0)
    return value.astype(BF16).astype(F32)


def kernel(
    sci_hbm, tmpl_hbm, own_hbm, pat_hbm, shf_hbm, frc_hbm, cof_hbm, kmain_hbm, kedge_hbm, kcol_hbm,
    diff, stack,
    sci, tmpl, own, pat, shf, frc, cof, kmain, kedge, kcol,
    req_out, req_in, meta_fwd, meta_out, meta_in, send_buf, fetch, warp_op, taps_fwd, taps_bwd, slot_img,
    img, halo_rows, across, col_op, acc, low, back_out, back_in, back_op,
    load_sem, req_send, req_recv, meta_send, meta_recv, tmpl_send, tmpl_recv,
    halo_send, halo_recv, back_send, back_recv,
    *, capacity,
):
    n = lax.axis_size("ccd")
    rows_n = lax.axis_size("row")
    cols_n = lax.axis_size("amp")
    me = lax.axis_index("ccd")
    my_row = lax.axis_index("row")
    my_col = lax.axis_index("amp")
    strips, srows, width = tmpl.shape
    band = strips * srows
    span = capacity * srows
    slots = n * capacity
    padded = width + 2 * LANES

    def peer(d):
        return {"ccd": lax.rem(me + d, n)}

    def back_peer(d):
        return {"ccd": lax.rem(me + n - d, n)}

    loads = [
        pltpu.make_async_copy(src, dst, load_sem.at[i])
        for i, (src, dst) in enumerate(
            [(own_hbm, own), (pat_hbm, pat), (shf_hbm, shf), (frc_hbm, frc), (cof_hbm, cof),
             (tmpl_hbm, tmpl), (kmain_hbm, kmain), (kedge_hbm, kedge), (kcol_hbm, kcol), (sci_hbm, sci)]
        )
    ]
    for load in loads:
        load.start()

    other_row = 1 - 2 * my_row
    other_col = 1 - 2 * my_col
    if rows_n == 2:
        steps = [(other_row, 0), (0, other_col), (other_row, other_col)]
    else:
        steps = [(-1, 0), (1, 0), (0, other_col), (-1, other_col), (1, other_col)]

    def when(step):
        if rows_n == 2 or (not isinstance(step[0], int)) or step[0] == 0:
            return lambda run: run()
        return pl.when((my_row + step[0] >= 0) & (my_row + step[0] < rows_n))

    def neighbour(step):
        return {"row": my_row + step[0], "amp": my_col + step[1]}

    barrier = pltpu.get_barrier_semaphore()
    for d in range(1, n):
        pl.semaphore_signal(barrier, inc=1, device_id=peer(d), device_id_type=MESH)
    for step in steps:
        @when(step)
        def _():
            pl.semaphore_signal(barrier, inc=1, device_id=neighbour(step), device_id_type=MESH)

    loads[0].wait()
    loads[1].wait()
    owner = [own[0, q] for q in range(strips)]
    slot_of = []
    for q in range(strips):
        rank = jnp.int32(0)
        for e in range(q):
            rank = rank + jnp.where(owner[e] == owner[q], 1, 0)
        away = owner[q] - me
        away = jnp.where(away < 0, away + n, away)
        slot_of.append(jnp.minimum(away * capacity + rank, slots - 1))
    strip_of = []
    wanted = []
    for s in range(slots):
        q_at = jnp.int32(-1)
        for q in range(strips):
            q_at = jnp.where(slot_of[q] == s, q, q_at)
        q_in = jnp.maximum(q_at, 0)
        strip_of.append(q_in)
        wanted.append(jnp.where(q_at < 0, -1, pat[0, q_in]))
    for d in range(1, n):
        for r in range(capacity):
            req_out[d, r] = jnp.maximum(wanted[d * capacity + r], 0)

    if rows_n == 2:
        around = n - 1 + len(steps)
    else:
        ends = jnp.where(my_row == 0, 1, 0) + jnp.where(my_row == rows_n - 1, 1, 0)
        around = n - 1 + len(steps) - 2 * ends
    pl.semaphore_wait(barrier, around)

    def request(d):
        return pltpu.make_async_remote_copy(
            src_ref=req_out.at[d], dst_ref=req_in.at[d], send_sem=req_send.at[d], recv_sem=req_recv.at[d],
            device_id=peer(d), device_id_type=MESH)

    for d in range(1, n):
        request(d).start()

    loads[5].wait()
    for r in range(capacity):
        fetch[0, r * srows:(r + 1) * srows, :] = tmpl[jnp.maximum(wanted[r], 0)]

    def reply(d):
        return pltpu.make_async_remote_copy(
            src_ref=send_buf.at[d], dst_ref=fetch.at[d], send_sem=tmpl_send.at[d], recv_sem=tmpl_recv.at[d],
            device_id=back_peer(d), device_id_type=MESH)

    for d in range(1, n):
        request(d).wait_recv()
        for r in range(capacity):
            send_buf[d, r * srows:(r + 1) * srows, :] = tmpl[req_in[d, r]]
        reply(d).start()

    lane = lax.broadcasted_iota(jnp.int32, (8, LANES), 1)
    sub = lax.broadcasted_iota(jnp.int32, (8, LANES), 0)
    tap = (sub - 2).astype(F32)

    def meta(d):
        return pltpu.make_async_remote_copy(
            src_ref=meta_out.at[d], dst_ref=meta_in.at[d], send_sem=meta_send.at[d], recv_sem=meta_recv.at[d],
            device_id=peer(d), device_id_type=MESH)

    for i in range(2, 4):
        loads[i].wait()

    def meta_table(d, rank):
        frac = jnp.full((8, LANES), 0.5, F32)
        shift = jnp.zeros((8, LANES), F32)
        which = jnp.full((8, LANES), -1.0, F32)
        for r in range(capacity):
            s = d * capacity + r
            frac = jnp.where(rank == r, frc[0, strip_of[s]], frac)
            shift = jnp.where(rank == r, shf[0, strip_of[s]].astype(F32), shift)
            which = jnp.where(rank == r, wanted[s].astype(F32), which)
        taps = taps_of(tap - frac)
        return jnp.where(sub == 6, shift, jnp.where(sub == 7, which, taps))

    part_rows = srows // 2
    for d in list(range(1, n)) + [0]:
        meta_out[d] = meta_table(d, lax.rem(lane // part_rows, capacity))
        if d:
            meta(d).start()
    for d in range(n):
        meta_fwd[d] = meta_table(d, lane // srows)

    row_at = lax.broadcasted_iota(jnp.int32, (srows, LANES), 0)
    lane_at = lax.broadcasted_iota(jnp.int32, (srows, LANES), 1)
    lane_in = lax.rem(lane_at, srows)

    def place(table, offset):
        total = jnp.zeros((srows, LANES), F32)
        for t in range(6):
            total = jnp.where(offset == t - 2, table[t:t + 1, :], total)
        return total

    for d in range(n):
        table = meta_fwd[d]
        shift = table[6:7, :].astype(jnp.int32)
        operator = place(table, lane_in - row_at - shift)
        for r in range(capacity):
            mine = (lane_at >= r * srows) & (lane_at < (r + 1) * srows)
            warp_op[d, r * srows:(r + 1) * srows, :] = jnp.where(mine, operator, 0.0).astype(BF16)

    col_at = lax.broadcasted_iota(jnp.int32, (8, width), 1)
    tap_at = lax.broadcasted_iota(jnp.int32, (8, width), 0) - 2
    for s in range(slots):
        taps = taps_of(tap - frc[1, strip_of[s]])
        wide = jnp.concatenate([taps] * (width // LANES), axis=1)
        moved = tap_at + shf[1, strip_of[s]]
        ahead, behind = col_at + moved, col_at - moved
        taps_fwd[s] = jnp.where((ahead >= 0) & (ahead < width), wide, 0.0)
        taps_bwd[s] = jnp.where((behind >= 0) & (behind < width), wide, 0.0)

    for i in (4, 6, 7, 8):
        loads[i].wait()
    halves = width // TILE
    window = 2 * TILE
    first = LANES - EDGE
    last = LANES + TILE + EDGE
    place_x = lax.broadcasted_iota(jnp.int32, (1, TILE), 1).astype(F32) + (my_col * width).astype(F32)
    for h in range(halves):
        for a in range(3):
            col_op[h, a * window:a * window + first, :] = jnp.zeros((first, 2 * TILE), BF16)
            col_op[h, a * window + last:(a + 1) * window, :] = jnp.zeros((window - last, 2 * TILE), BF16)
    chunk = 48
    for a in range(3):
        @pl.loop(0, (last - first) // chunk)
        def _(i):
            at = pl.ds(pl.multiple_of(i * chunk, 16), chunk)
            base = [kcol[b, at, :].astype(F32) for b in range(3)]
            fold = [
                cof[j, 0, 3 * a] * base[0] + cof[j, 0, 3 * a + 1] * base[1] + cof[j, 0, 3 * a + 2] * base[2]
                for j in range(3)
            ]
            to = pl.ds(pl.multiple_of(a * window + first + i * chunk, 16), chunk)
            for h in range(halves):
                px = (place_x + (h * TILE + 0.5)) / (width * cols_n) * 2.0 - 1.0
                col_op[h, to, 0:TILE] = (fold[0] + px * fold[1]).astype(BF16)
                col_op[h, to, TILE:] = fold[2].astype(BF16)

    if rows_n == 2:
        halves_at = [pl.multiple_of(part_rows * my_row, part_rows), pl.multiple_of(part_rows * (1 - my_row), part_rows)]
    else:
        halves_at = [0, part_rows]
    part_span = capacity * part_rows
    group = LANES // part_span
    for g in range(n // group):
        for e in range(group):
            d = g * group + e
            if d:
                meta(d).wait_recv()
            came = meta_in[d] if d else meta_out[0]
            table = came if e == 0 else jnp.where(lane // part_span == e, came, table)
        shift = table[6:7, :].astype(jnp.int32)
        which = table[7:8, :].astype(jnp.int32)
        for part in range(2):
            operator = place(table, row_at - (lax.rem(lane_at, part_rows) + halves_at[part]) - shift)
            for p in range(strips):
                back_op[part, p * srows:(p + 1) * srows, g * LANES:(g + 1) * LANES] = jnp.where(which == p, operator, 0.0).astype(BF16)

    right = LANES + width
    col_in = pl.multiple_of(jnp.where(my_col == 0, right, 0), LANES)
    col_out = pl.multiple_of(jnp.where(my_col == 0, 0, right), LANES)
    img[:, pl.ds(col_out, LANES)] = jnp.zeros((band, LANES), BF16)
    halo_rows[:, :, pl.ds(col_out, LANES)] = jnp.zeros((2, EDGE, LANES), BF16)
    if rows_n > 2:
        @pl.when(my_row == 0)
        def _():
            halo_rows[0] = jnp.zeros((EDGE, padded), BF16)

        @pl.when(my_row == rows_n - 1)
        def _():
            halo_rows[1] = jnp.zeros((EDGE, padded), BF16)
    edge_col = [pl.multiple_of(a * window + jnp.where(my_col == 0, window - LANES, 0), LANES) for a in range(3)]
    for a in range(3):
        far_col = pl.multiple_of(a * window + jnp.where(my_col == 0, 0, window - LANES), LANES)
        across[my_col * (halves - 1), :, pl.ds(far_col, LANES)] = jnp.zeros((band, LANES), BF16)

    for d in range(n):
        if d:
            reply(d).wait_recv()
        rows_done = jnp.dot(warp_op[d, :, :span], fetch[d], preferred_element_type=F32).astype(BF16)
        for r in range(capacity):
            s = d * capacity + r
            value = rows_done[r * srows:(r + 1) * srows, :]
            move = shf[1, strip_of[s]]
            total = jnp.zeros((srows, width), F32)
            for t in range(6):
                moved = pltpu.roll(value, width - (move + (t - 2)), 1).astype(F32)
                total = total + taps_fwd[s, t:t + 1, :] * moved
            slot_img[s] = total.astype(BF16)
    for q in range(strips):
        img[q * srows:(q + 1) * srows, LANES:right] = slot_img[slot_of[q]]

    def halo(i):
        step = steps[i]
        if isinstance(step[1], int):
            cols_src = cols_dst = pl.ds(LANES, width)
        else:
            cols_src = pl.ds(pl.multiple_of(jnp.where(my_col == 0, right - LANES, LANES), LANES), LANES)
            cols_dst = pl.ds(col_out, LANES)
        if isinstance(step[0], int) and step[0] == 0:
            src, dst = img.at[:, cols_src], img.at[:, cols_dst]
        elif isinstance(step[0], int):
            top = band - EDGE if step[0] > 0 else 0
            src = img.at[pl.ds(top, EDGE), cols_src]
            dst = halo_rows.at[0 if step[0] > 0 else 1, :, cols_dst]
        else:
            top = pl.multiple_of(jnp.where(my_row == 0, band - EDGE, 0), EDGE)
            src = img.at[pl.ds(top, EDGE), cols_src]
            dst = halo_rows.at[my_row, :, cols_dst]
        return pltpu.make_async_remote_copy(
            src_ref=src, dst_ref=dst, send_sem=halo_send.at[i], recv_sem=halo_recv.at[i],
            device_id=neighbour(step), device_id_type=MESH)

    for i, step in enumerate(steps):
        @when(step)
        def _(i=i):
            halo(i).start()

    def put(a, row, count, col, value):
        value = value.astype(BF16)
        for h in range(halves):
            begin, end = h * TILE, h * TILE + window
            lo, hi = max(begin, col), min(end, col + value.shape[1])
            if lo < hi:
                across[h, pl.ds(row, count), a * window + lo - begin:a * window + hi - begin] = value[:, lo - col:hi - col]

    for c in range(width // TILE):
        col = LANES + c * TILE
        for a in range(3):
            part = jnp.dot(kmain[a * band:(a + 1) * band, :], img[:, col:col + TILE], preferred_element_type=F32)
            put(a, 0, band, col, part)

    def received(step):
        if isinstance(step[0], int):
            return (-step[0], step[1])
        return step

    def await_halo(at):
        @when(received(steps[at]))
        def _():
            halo(at).wait_recv()

    amp_at = [i for i, step in enumerate(steps) if isinstance(step[0], int) and step[0] == 0]
    row_at_steps = [i for i in range(len(steps)) if i not in amp_at]
    edge_half = (1 - my_col) * (halves - 1)

    def edge_columns():
        for i in amp_at:
            await_halo(i)
        for a in range(3):
            part = jnp.dot(kmain[a * band:(a + 1) * band, :], img[:, pl.ds(col_in, LANES)], preferred_element_type=F32)
            across[edge_half, :, pl.ds(edge_col[a], LANES)] = part.astype(BF16)

    def edge_rows():
        for i in row_at_steps:
            await_halo(i)
        if rows_n == 2:
            edges = [(1 - my_row, pl.multiple_of(jnp.where(my_row == 0, band - EDGE, 0), EDGE))]
        else:
            edges = [(0, 0), (1, band - EDGE)]
        for a in range(3):
            for side, top in edges:
                near = kmain[pl.ds(pl.multiple_of(a * band + top, EDGE), EDGE), :]
                total = jnp.dot(near, img[...], preferred_element_type=F32)
                total = total + jnp.dot(kedge[side, a], halo_rows[side], preferred_element_type=F32)
                put(a, top, EDGE, 0, total)

    def rows_of(part, q):
        return pl.ds(pl.multiple_of(q * srows + halves_at[part], part_rows), part_rows)

    half_rows = strips * part_rows

    def subtract(part, half):
        lhs = jnp.concatenate([across[half, rows_of(part, q), :] for q in range(strips)], axis=0)
        acc[...] = jnp.dot(lhs, col_op[half], preferred_element_type=F32)
        at = pl.ds(pl.multiple_of(half * TILE, TILE), TILE)
        local = lax.broadcasted_iota(jnp.int32, (part_rows, TILE), 0)
        for q in range(strips):
            y = local + (my_row * band + q * srows + halves_at[part])
            py = (y.astype(F32) + 0.5) / (band * rows_n) * 2.0 - 1.0
            rows = slice(q * part_rows, (q + 1) * part_rows)
            value = sci[rows_of(part, q), at] - (acc[rows, 0:TILE] + py * acc[rows, TILE:])
            diff[rows_of(part, q), at] = value
            low[q, pl.ds(halves_at[part], part_rows), at] = value.astype(BF16)

    def give(d, part):
        at = pl.ds(d * part_span, part_span)
        return pltpu.make_async_remote_copy(
            src_ref=back_out.at[part, at], dst_ref=back_in.at[part, at],
            send_sem=back_send.at[part, d], recv_sem=back_recv.at[part, d],
            device_id=peer(d), device_id_type=MESH)

    def columns_back(part):
        for d in list(range(1, n)) + [0]:
            target = back_out if d else back_in
            for r in range(capacity):
                s = d * capacity + r
                value = low[strip_of[s], pl.ds(halves_at[part], part_rows), :]
                move = shf[1, strip_of[s]]
                total = jnp.zeros((part_rows, width), F32)
                for t in range(6):
                    moved = pltpu.roll(value, width + (move + (t - 2)), 1).astype(F32)
                    total = total + taps_bwd[s, t:t + 1, :] * moved
                target[part, d * part_span + r * part_rows:d * part_span + (r + 1) * part_rows, :] = total.astype(BF16)
            if d:
                give(d, part).start()

    loads[9].wait()
    if rows_n > 2:
        edge_columns()
        edge_rows()
    subtract(0, my_col * (halves - 1))
    if rows_n == 2:
        edge_columns()
    subtract(0, edge_half)
    columns_back(0)
    if rows_n == 2:
        edge_rows()
    subtract(1, my_col * (halves - 1))
    subtract(1, edge_half)
    columns_back(1)

    for part in range(2):
        for d in range(1, n):
            give(d, part).wait_recv()
        total = jnp.dot(back_op[part], back_in[part], preferred_element_type=F32)
        stack[...] = total if part == 0 else stack[...] + total

    for d in range(1, n):
        request(d).wait_send()
        reply(d).wait_send()
        meta(d).wait_send()
        give(d, 0).wait_send()
        give(d, 1).wait_send()
    for i, step in enumerate(steps):
        @when(step)
        def _(i=i):
            halo(i).wait_send()


def keep(diff, stack, diff_out, stack_out, sem):
    copies = [
        pltpu.make_async_copy(diff, diff_out, sem.at[0]),
        pltpu.make_async_copy(stack, stack_out, sem.at[1]),
    ]
    for copy in copies:
        copy.start()
    for copy in copies:
        copy.wait()


def body(science, template, owners, patch_strip, shifts, fractions, coefs):
    n = lax.axis_size("ccd")
    band, width = science.shape[1:]
    strips, srows = template.shape[3:5]
    capacity = max(2, strips // n)
    slots = n * capacity
    span = capacity * srows
    padded = width + 2 * LANES
    window = 2 * TILE
    halves = width // TILE
    kmain, kedge, kcol = conv_constants(band, window)
    hbm_spec = pl.BlockSpec(memory_space=pltpu.HBM)
    dma = pltpu.SemaphoreType.DMA
    scratch = [
        pltpu.VMEM((band, width), F32),
        pltpu.VMEM((strips, srows, width), BF16),
        pltpu.SMEM((1, strips), jnp.int32),
        pltpu.SMEM((1, strips), jnp.int32),
        pltpu.SMEM((2, strips), jnp.int32),
        pltpu.SMEM((2, strips), F32),
        pltpu.SMEM((3, 1, 9), F32),
        pltpu.VMEM(kmain.shape, BF16),
        pltpu.VMEM(kedge.shape, BF16),
        pltpu.VMEM(kcol.shape, BF16),
        pltpu.SMEM((n, LANES), jnp.int32),
        pltpu.SMEM((n, LANES), jnp.int32),
        pltpu.VMEM((n, 8, LANES), F32),
        pltpu.VMEM((n, 8, LANES), F32),
        pltpu.VMEM((n, 8, LANES), F32),
        pltpu.VMEM((n, span, width), BF16),
        pltpu.VMEM((n, span, width), BF16),
        pltpu.VMEM((n, span, LANES), BF16),
        pltpu.VMEM((slots, 8, width), F32),
        pltpu.VMEM((slots, 8, width), F32),
        pltpu.VMEM((slots, srows, width), BF16),
        pltpu.VMEM((band, padded), BF16),
        pltpu.VMEM((2, EDGE, padded), BF16),
        pltpu.VMEM((halves, band, 3 * window), BF16),
        pltpu.VMEM((halves, 3 * window, 2 * TILE), BF16),
        pltpu.VMEM((band // 2, 2 * TILE), F32),
        pltpu.VMEM((strips, srows, width), BF16),
        pltpu.VMEM((2, n * span // 2, width), BF16),
        pltpu.VMEM((2, n * span // 2, width), BF16),
        pltpu.VMEM((2, band, n * span // 2), BF16),
        dma((10,)),
        dma((n,)), dma((n,)), dma((n,)), dma((n,)), dma((n,)), dma((n,)),
        dma((8,)), dma((8,)),
        dma((2, n)), dma((2, n)),
    ]
    difference, stack = pl.pallas_call(
        functools.partial(kernel, capacity=capacity),
        out_shape=(
            jax.ShapeDtypeStruct((band, width), F32),
            jax.ShapeDtypeStruct((band, width), F32),
        ),
        in_specs=[hbm_spec] * 10,
        out_specs=(pl.BlockSpec(memory_space=pltpu.VMEM),) * 2,
        scratch_shapes=scratch,
        compiler_params=pltpu.CompilerParams(
            collective_id=0, has_side_effects=True, vmem_limit_bytes=40 * 1024 * 1024
        ),
    )(
        pltpu.with_memory_space_constraint(science[0], pltpu.HBM),
        pltpu.with_memory_space_constraint(template.reshape(strips, srows, width), pltpu.HBM),
        pltpu.with_memory_space_constraint(owners.reshape(1, strips), pltpu.HBM),
        pltpu.with_memory_space_constraint(patch_strip.reshape(1, strips), pltpu.HBM),
        pltpu.with_memory_space_constraint(shifts.reshape(2, strips), pltpu.HBM),
        pltpu.with_memory_space_constraint(fractions.reshape(2, strips), pltpu.HBM),
        pltpu.with_memory_space_constraint(coefs.transpose(1, 0, 2), pltpu.HBM),
        pltpu.with_memory_space_constraint(jnp.asarray(kmain), pltpu.HBM),
        pltpu.with_memory_space_constraint(jnp.asarray(kedge), pltpu.HBM),
        pltpu.with_memory_space_constraint(jnp.asarray(kcol), pltpu.HBM),
    )
    difference, stack = pl.pallas_call(
        keep,
        out_shape=(
            jax.ShapeDtypeStruct((band, width), F32),
            jax.ShapeDtypeStruct((band, width), F32),
        ),
        in_specs=[pl.BlockSpec(memory_space=pl.ANY)] * 2,
        out_specs=(hbm_spec, hbm_spec),
        scratch_shapes=[dma((2,))],
    )(
        pltpu.with_memory_space_constraint(difference, pltpu.VMEM),
        pltpu.with_memory_space_constraint(stack, pltpu.VMEM),
    )
    return difference[None], stack.reshape(template.shape)


def solution(mesh):
    return jax.shard_map(
        body,
        mesh=mesh,
        in_specs=(
            P(("grp", "ccd"), "row", "amp"),
            P(("grp", "ccd"), "row", "amp", None, None, None),
            P(("grp", "ccd"), "row", "amp", None, None),
            P(("grp", "ccd"), "row", "amp", None),
            P(("grp", "ccd"), "row", "amp", None, None),
            P(("grp", "ccd"), "row", "amp", None, None),
            P(("grp", "ccd"), None, None),
        ),
        out_specs=(
            P(("grp", "ccd"), "row", "amp"),
            P(("grp", "ccd"), "row", "amp", None, None, None),
        ),
        check_vma=False,
    )
```

```python
import functools

import jax
import jax.numpy as jnp
import ml_dtypes
import numpy as np
from jax import lax
from jax.experimental import pallas as pl
from jax.experimental.pallas import tpu as pltpu
from jax.sharding import PartitionSpec as P

RADIUS = 9
EDGE = 16
LANES = 128
TILE = 256
MESH = pl.DeviceIdType.MESH
F32 = jnp.float32
BF16 = jnp.bfloat16


def kernel_table():
    support = np.arange(-RADIUS, RADIUS + 1).astype(np.float32)
    narrow = np.exp(-support * support / np.float32(4.5))
    slope = support * np.exp(-support * support / np.float32(12.5))
    broad = np.exp(-support * support / np.float32(40.5))
    table = np.stack(
        [narrow / np.sum(narrow), slope / np.sum(np.abs(slope)), broad / np.sum(broad)]
    )
    return table.astype(ml_dtypes.bfloat16)


def toeplitz(kernel, out_at, in_at):
    offset = in_at[None, :] - out_at[:, None] + RADIUS
    inside = (offset >= 0) & (offset <= 2 * RADIUS)
    return np.where(inside, kernel[np.clip(offset, 0, 2 * RADIUS)], np.zeros((), kernel.dtype))


def conv_constants(rows):
    table = kernel_table()
    at = np.arange(rows)
    main = np.concatenate([toeplitz(k, at, at) for k in table], axis=0)
    top = np.stack([toeplitz(k, np.arange(EDGE), np.arange(-EDGE, 0)) for k in table])
    bottom = np.stack(
        [toeplitz(k, np.arange(-EDGE, 0), np.arange(EDGE)) for k in table]
    )
    source = np.arange(-EDGE, LANES + EDGE)
    cols = np.stack([toeplitz(k, np.arange(LANES), source).T for k in table])
    return main, np.stack([top, bottom]), cols


def sinc(value):
    angle = np.float32(np.pi) * value
    return jnp.sin(angle) / angle


def taps_of(offset):
    value = sinc(offset) * sinc(offset / 3.0)
    return value.astype(BF16).astype(F32)


def kernel(
    sci_hbm, tmpl_hbm, own_hbm, pat_hbm, shf_hbm, frc_hbm, cof_hbm, kmain_hbm, kedge_hbm, kcol_hbm,
    diff, stack,
    sci, tmpl, own, pat, shf, frc, cof, kmain, kedge, kcol,
    req_out, req_in, meta_out, meta_in, send_buf, fetch, warp_op, taps_fwd, taps_bwd, slot_img,
    img, halo_rows, across, col_op, acc, low, back_free, back_late, back_in, back_op,
    load_sem, req_send, req_recv, meta_send, meta_recv, tmpl_send, tmpl_recv,
    halo_send, halo_recv, back_send, back_recv,
    *, capacity,
):
    n = lax.axis_size("ccd")
    rows_n = lax.axis_size("row")
    cols_n = lax.axis_size("amp")
    me = lax.axis_index("ccd")
    my_row = lax.axis_index("row")
    my_col = lax.axis_index("amp")
    strips, srows, width = tmpl.shape
    band = strips * srows
    span = capacity * srows
    slots = n * capacity
    padded = width + 2 * LANES

    def peer(d):
        return {"ccd": lax.rem(me + d, n)}

    def back_peer(d):
        return {"ccd": lax.rem(me + n - d, n)}

    loads = [
        pltpu.make_async_copy(src, dst, load_sem.at[i])
        for i, (src, dst) in enumerate(
            [(own_hbm, own), (pat_hbm, pat), (shf_hbm, shf), (frc_hbm, frc), (cof_hbm, cof),
             (tmpl_hbm, tmpl), (kmain_hbm, kmain), (kedge_hbm, kedge), (kcol_hbm, kcol), (sci_hbm, sci)]
        )
    ]
    for load in loads:
        load.start()

    other_row = 1 - 2 * my_row
    other_col = 1 - 2 * my_col
    if rows_n == 2:
        steps = [(0, other_col), (other_row, 0), (other_row, other_col)]
    else:
        steps = [(-1, 0), (1, 0), (0, other_col), (-1, other_col), (1, other_col)]

    def when(step):
        if rows_n == 2 or (not isinstance(step[0], int)) or step[0] == 0:
            return lambda run: run()
        return pl.when((my_row + step[0] >= 0) & (my_row + step[0] < rows_n))

    def neighbour(step):
        return {"row": my_row + step[0], "amp": my_col + step[1]}

    barrier = pltpu.get_barrier_semaphore()
    for d in range(1, n):
        pl.semaphore_signal(barrier, inc=1, device_id=peer(d), device_id_type=MESH)
    for step in steps:
        @when(step)
        def _():
            pl.semaphore_signal(barrier, inc=1, device_id=neighbour(step), device_id_type=MESH)

    loads[0].wait()
    loads[1].wait()
    owner = [own[0, q] for q in range(strips)]
    slot_of = []
    for q in range(strips):
        rank = jnp.int32(0)
        for e in range(q):
            alike = owner[e] == owner[q]
            rank = rank + jnp.where(alike & (my_row == 0) if e == 0 else alike, 1, 0)
        if q == 0:
            rank = jnp.where(my_row == 0, rank, capacity - 1)
        if q == strips - 1:
            rank = jnp.where(my_row == 0, capacity - 1, rank)
        away = owner[q] - me
        away = jnp.where(away < 0, away + n, away)
        slot_of.append(jnp.minimum(away * capacity + rank, slots - 1))
    strip_of = []
    wanted = []
    for s in range(slots):
        q_at = jnp.int32(-1)
        for q in range(strips):
            q_at = jnp.where(slot_of[q] == s, q, q_at)
        q_in = jnp.maximum(q_at, 0)
        strip_of.append(q_in)
        wanted.append(jnp.where(q_at < 0, -1, pat[0, q_in]))
    for d in range(1, n):
        for r in range(capacity):
            req_out[d, r] = jnp.maximum(wanted[d * capacity + r], 0)

    if rows_n == 2:
        around = n - 1 + len(steps)
    else:
        ends = jnp.where(my_row == 0, 1, 0) + jnp.where(my_row == rows_n - 1, 1, 0)
        around = n - 1 + len(steps) - 2 * ends
    pl.semaphore_wait(barrier, around)

    def request(d):
        return pltpu.make_async_remote_copy(
            src_ref=req_out.at[d], dst_ref=req_in.at[d], send_sem=req_send.at[d], recv_sem=req_recv.at[d],
            device_id=peer(d), device_id_type=MESH)

    for d in range(1, n):
        request(d).start()

    loads[5].wait()
    for r in range(capacity):
        fetch[r] = tmpl[jnp.maximum(wanted[r], 0)]

    def reply(d, r):
        s = d * capacity + r
        return pltpu.make_async_remote_copy(
            src_ref=send_buf.at[s], dst_ref=fetch.at[s], send_sem=tmpl_send.at[s], recv_sem=tmpl_recv.at[s],
            device_id=back_peer(d), device_id_type=MESH)

    for d in range(1, n):
        request(d).wait_recv()
        for r in range(capacity):
            send_buf[d * capacity + r] = tmpl[req_in[d, r]]
        reply(d, 0).start()
    for r in range(1, capacity):
        for d in range(1, n):
            reply(d, r).start()

    lane = lax.broadcasted_iota(jnp.int32, (8, LANES), 1)
    sub = lax.broadcasted_iota(jnp.int32, (8, LANES), 0)
    tap = (sub - 2).astype(F32)

    def meta(d):
        return pltpu.make_async_remote_copy(
            src_ref=meta_out.at[d], dst_ref=meta_in.at[d], send_sem=meta_send.at[d], recv_sem=meta_recv.at[d],
            device_id=peer(d), device_id_type=MESH)

    for i in range(2, 4):
        loads[i].wait()

    def slot_table(s):
        taps = taps_of(tap - frc[0, strip_of[s]])
        return taps, shf[0, strip_of[s]]

    def meta_table(d, rank):
        frac = jnp.full((8, LANES), 0.5, F32)
        shift = jnp.zeros((8, LANES), F32)
        which = jnp.full((8, LANES), -1.0, F32)
        for r in range(capacity):
            s = d * capacity + r
            frac = jnp.where(rank == r, frc[0, strip_of[s]], frac)
            shift = jnp.where(rank == r, shf[0, strip_of[s]].astype(F32), shift)
            which = jnp.where(rank == r, wanted[s].astype(F32), which)
        taps = taps_of(tap - frac)
        return jnp.where(sub == 6, shift, jnp.where(sub == 7, which, taps))

    part_rows = srows // 2
    for d in list(range(1, n)) + [0]:
        meta_out[d] = meta_table(d, lax.rem(lane // srows, capacity))
        if d:
            meta(d).start()

    row_at = lax.broadcasted_iota(jnp.int32, (srows, LANES), 0)
    lane_at = lax.broadcasted_iota(jnp.int32, (srows, LANES), 1)

    def place(table, offset):
        total = jnp.zeros((srows, LANES), F32)
        for t in range(6):
            total = jnp.where(offset == t - 2, table[t:t + 1, :], total)
        return total

    for s in range(slots):
        taps, shift = slot_table(s)
        warp_op[s] = place(taps, lane_at - row_at - shift).astype(BF16)

    col_at = lax.broadcasted_iota(jnp.int32, (8, width), 1)
    tap_at = lax.broadcasted_iota(jnp.int32, (8, width), 0) - 2
    for s in range(slots):
        taps = taps_of(tap - frc[1, strip_of[s]])
        wide = jnp.concatenate([taps] * (width // LANES), axis=1)
        moved = tap_at + shf[1, strip_of[s]]
        ahead, behind = col_at + moved, col_at - moved
        taps_fwd[s] = jnp.where((ahead >= 0) & (ahead < width), wide, 0.0)
        taps_bwd[s] = jnp.where((behind >= 0) & (behind < width), wide, 0.0)

    for i in (4, 6, 7, 8):
        loads[i].wait()
    tiles = width // LANES
    window = 3 * LANES
    first = LANES - EDGE
    last = 2 * LANES + EDGE
    place_x = lax.broadcasted_iota(jnp.int32, (1, LANES), 1).astype(F32) + (my_col * width).astype(F32)
    for j in range(tiles):
        for a in range(3):
            col_op[j, a * window:a * window + first, :] = jnp.zeros((first, 2 * LANES), BF16)
            col_op[j, a * window + last:(a + 1) * window, :] = jnp.zeros((window - last, 2 * LANES), BF16)
    chunk = 80
    for a in range(3):
        @pl.loop(0, (last - first) // chunk)
        def _(i):
            at = pl.ds(pl.multiple_of(i * chunk, 16), chunk)
            base = [kcol[b, at, :].astype(F32) for b in range(3)]
            fold = [
                cof[j, 0, 3 * a] * base[0] + cof[j, 0, 3 * a + 1] * base[1] + cof[j, 0, 3 * a + 2] * base[2]
                for j in range(3)
            ]
            to = pl.ds(pl.multiple_of(a * window + first + i * chunk, 16), chunk)
            for j in range(tiles):
                px = (place_x + (j * LANES + 0.5)) / (width * cols_n) * 2.0 - 1.0
                col_op[j, to, 0:LANES] = (fold[0] + px * fold[1]).astype(BF16)
                col_op[j, to, LANES:] = fold[2].astype(BF16)

    if rows_n == 2:
        halves_at = [pl.multiple_of(part_rows * my_row, part_rows), pl.multiple_of(part_rows * (1 - my_row), part_rows)]
    else:
        halves_at = [0, part_rows]
    late = part_rows
    free = span - late
    group = LANES // span

    right = LANES + width
    col_in = pl.multiple_of(jnp.where(my_col == 0, right, 0), LANES)
    col_out = pl.multiple_of(jnp.where(my_col == 0, 0, right), LANES)
    img[:, pl.ds(col_out, LANES)] = jnp.zeros((band, LANES), BF16)
    halo_rows[:, :, pl.ds(col_out, LANES)] = jnp.zeros((2, EDGE, LANES), BF16)
    if rows_n > 2:
        @pl.when(my_row == 0)
        def _():
            halo_rows[0] = jnp.zeros((EDGE, padded), BF16)

        @pl.when(my_row == rows_n - 1)
        def _():
            halo_rows[1] = jnp.zeros((EDGE, padded), BF16)
    for a in range(3):
        across[a, :, pl.ds(col_out, LANES)] = jnp.zeros((band, LANES), BF16)

    for r in range(capacity):
        for d in range(n):
            s = d * capacity + r
            if d:
                reply(d, r).wait_recv()
            value = jnp.dot(warp_op[s, :, :srows], fetch[s], preferred_element_type=F32).astype(BF16)
            move = shf[1, strip_of[s]]
            total = jnp.zeros((srows, width), F32)
            for t in range(6):
                moved = pltpu.roll(value, width - (move + (t - 2)), 1).astype(F32)
                total = total + taps_fwd[s, t:t + 1, :] * moved
            slot_img[s] = total.astype(BF16)
    for q in range(strips):
        img[q * srows:(q + 1) * srows, LANES:right] = slot_img[slot_of[q]]

    def halo(i):
        step = steps[i]
        if isinstance(step[1], int):
            cols_src = cols_dst = pl.ds(LANES, width)
        else:
            cols_src = pl.ds(pl.multiple_of(jnp.where(my_col == 0, right - LANES, LANES), LANES), LANES)
            cols_dst = pl.ds(col_out, LANES)
        if isinstance(step[0], int) and step[0] == 0:
            src, dst = img.at[:, cols_src], img.at[:, cols_dst]
        elif isinstance(step[0], int):
            top = band - EDGE if step[0] > 0 else 0
            src = img.at[pl.ds(top, EDGE), cols_src]
            dst = halo_rows.at[0 if step[0] > 0 else 1, :, cols_dst]
        else:
            top = pl.multiple_of(jnp.where(my_row == 0, band - EDGE, 0), EDGE)
            src = img.at[pl.ds(top, EDGE), cols_src]
            dst = halo_rows.at[my_row, :, cols_dst]
        return pltpu.make_async_remote_copy(
            src_ref=src, dst_ref=dst, send_sem=halo_send.at[i], recv_sem=halo_recv.at[i],
            device_id=neighbour(step), device_id_type=MESH)

    for i, step in enumerate(steps):
        @when(step)
        def _(i=i):
            halo(i).start()

    def received(step):
        if isinstance(step[0], int):
            return (-step[0], step[1])
        return step

    def await_halo(at):
        @when(received(steps[at]))
        def _():
            halo(at).wait_recv()

    def across_of(col, count):
        for a in range(3):
            total = jnp.dot(kmain[a * band:(a + 1) * band, :], img[:, pl.ds(col, count)], preferred_element_type=F32)
            across[a, :, pl.ds(col, count)] = total.astype(BF16)

    if rows_n == 2:
        edges = [(1 - my_row, pl.multiple_of(jnp.where(my_row == 0, band - EDGE, 0), EDGE))]
    else:
        edges = [(0, 0), (1, band - EDGE)]

    def edge_rows():
        for a in range(3):
            for side, top in edges:
                near = kmain[pl.ds(pl.multiple_of(a * band + top, EDGE), EDGE), :]
                total = jnp.dot(near, img[...], preferred_element_type=F32)
                total = total + jnp.dot(kedge[side, a], halo_rows[side], preferred_element_type=F32)
                across[a, pl.ds(top, EDGE), :] = total.astype(BF16)

    def subtract(turn, top, rows):
        tile = my_col * (tiles - 1) + turn * (1 - 2 * my_col)
        here = pl.ds(top, rows)
        at = pl.ds(pl.multiple_of(tile * LANES, LANES), window)
        lhs = jnp.concatenate([across[a, here, at] for a in range(3)], axis=1)
        acc[0:rows, :] = jnp.dot(lhs, col_op[tile], preferred_element_type=F32)
        at = pl.ds(pl.multiple_of(tile * LANES, LANES), LANES)
        step = min(rows, srows)
        local = lax.broadcasted_iota(jnp.int32, (step, LANES), 0)
        for q in range(rows // step):
            y = local + (my_row * band + top + q * step)
            py = (y.astype(F32) + 0.5) / (band * rows_n) * 2.0 - 1.0
            part = slice(q * step, (q + 1) * step)
            to = pl.ds(pl.multiple_of(top + q * step, step), step)
            value = sci[to, at] - (acc[part, 0:LANES] + py * acc[part, LANES:])
            diff[to, at] = value
            strip = top // srows + q
            low[strip, pl.ds(pl.multiple_of(top - top // srows * srows, step), step), at] = value.astype(BF16)

    piece_cols = width // 2
    region = piece_cols + LANES

    def piece_at(piece):
        inner = my_col if piece == 0 else 1 - my_col
        return pl.multiple_of(inner * piece_cols, LANES), pl.multiple_of(inner * LANES, LANES)

    def give(d, piece):
        if piece == 2:
            src = back_late.at[pl.ds(d * late, late)]
            dst = back_in.at[pl.ds(d * span + free, late)]
        else:
            at, offset = piece_at(piece)
            src = back_free.at[piece, pl.ds(d * free, free), pl.ds(offset, piece_cols)]
            dst = back_in.at[pl.ds(d * span, free), pl.ds(at, piece_cols)]
        return pltpu.make_async_remote_copy(
            src_ref=src, dst_ref=dst, send_sem=back_send.at[piece, d], recv_sem=back_recv.at[piece, d],
            device_id=peer(d), device_id_type=MESH)

    def column_sum(s, top, rows, source, cols):
        value = low[strip_of[s], pl.ds(top, rows), source]
        move = shf[1, strip_of[s]]
        total = jnp.zeros((rows, cols), F32)
        for t in range(6):
            moved = pltpu.roll(value, cols + (move + (t - 2)), 1).astype(F32)
            total = total + taps_bwd[s, t:t + 1, source] * moved
        return total.astype(BF16)

    def columns_back(piece):
        if piece < 2:
            at, offset = piece_at(piece)
            source = pl.ds(pl.multiple_of(at - offset, LANES), region)
        for d in list(range(1, n)) + [0]:
            if piece == 2:
                back_late[d * late:(d + 1) * late, :] = column_sum(
                    (d + 1) * capacity - 1, halves_at[1], late, pl.ds(0, width), width)
            else:
                for r in range(capacity):
                    rows = srows if r < capacity - 1 else srows - late
                    top = 0 if r < capacity - 1 else halves_at[0]
                    to = d * free + r * srows
                    back_free[piece, to:to + rows, :] = column_sum(d * capacity + r, top, rows, source, region)
            if d:
                give(d, piece).start()
        if piece == 2:
            back_in[free:span, :] = back_late[0:late, :]
        else:
            back_in[0:free, pl.ds(at, piece_cols)] = back_free[piece, 0:free, pl.ds(offset, piece_cols)]

    amp_at = [i for i, step in enumerate(steps) if isinstance(step[0], int) and step[0] == 0]
    row_at_steps = [i for i in range(len(steps)) if i not in amp_at]

    def finish_edges():
        for i in row_at_steps:
            await_halo(i)
        edge_rows()

    loads[9].wait()
    for c in range(width // TILE):
        across_of(pl.multiple_of(LANES + (c + (1 - 2 * c) * my_col) * TILE, LANES), TILE)
    if rows_n > 2:
        for i in amp_at:
            await_halo(i)
        across_of(col_in, LANES)
        finish_edges()
    for turn in range(tiles - 1):
        subtract(turn, 0, band)
    columns_back(0)
    if rows_n == 2:
        for i in amp_at:
            await_halo(i)
        across_of(col_in, LANES)
    subtract(tiles - 1, 0, band)
    columns_back(1)
    if rows_n == 2:
        finish_edges()
        for turn in range(tiles):
            subtract(turn, edges[0][1], EDGE)
    columns_back(2)

    span_at = lax.rem(lane_at, span)
    late_at = lax.rem(span_at, part_rows) + jnp.where(span_at < free, halves_at[0], halves_at[1])
    from_row = jnp.where(span_at < span - srows, lax.rem(span_at, srows), late_at)
    for g in range(n // group):
        for e in range(group):
            d = g * group + e
            if d:
                meta(d).wait_recv()
            came = meta_in[d] if d else meta_out[0]
            table = came if e == 0 else jnp.where(lane // span == e, came, table)
        shift = table[6:7, :].astype(jnp.int32)
        which = table[7:8, :].astype(jnp.int32)
        operator = place(table, row_at - from_row - shift)
        for p in range(strips):
            back_op[p * srows:(p + 1) * srows, g * LANES:(g + 1) * LANES] = jnp.where(which == p, operator, 0.0).astype(BF16)

    for piece in range(3):
        for d in range(1, n):
            give(d, piece).wait_recv()
    stack[...] = jnp.dot(back_op[...], back_in[...], preferred_element_type=F32)

    for d in range(1, n):
        request(d).wait_send()
        for r in range(capacity):
            reply(d, r).wait_send()
        meta(d).wait_send()
        for piece in range(3):
            give(d, piece).wait_send()
    for i, step in enumerate(steps):
        @when(step)
        def _(i=i):
            halo(i).wait_send()


def keep(diff, stack, diff_out, stack_out, sem):
    copies = [
        pltpu.make_async_copy(diff, diff_out, sem.at[0]),
        pltpu.make_async_copy(stack, stack_out, sem.at[1]),
    ]
    for copy in copies:
        copy.start()
    for copy in copies:
        copy.wait()


def body(science, template, owners, patch_strip, shifts, fractions, coefs):
    n = lax.axis_size("ccd")
    band, width = science.shape[1:]
    strips, srows = template.shape[3:5]
    capacity = max(2, strips // n)
    slots = n * capacity
    span = capacity * srows
    padded = width + 2 * LANES
    kmain, kedge, kcol = conv_constants(band)
    hbm_spec = pl.BlockSpec(memory_space=pltpu.HBM)
    dma = pltpu.SemaphoreType.DMA
    scratch = [
        pltpu.VMEM((band, width), F32),
        pltpu.VMEM((strips, srows, width), BF16),
        pltpu.SMEM((1, strips), jnp.int32),
        pltpu.SMEM((1, strips), jnp.int32),
        pltpu.SMEM((2, strips), jnp.int32),
        pltpu.SMEM((2, strips), F32),
        pltpu.SMEM((3, 1, 9), F32),
        pltpu.VMEM(kmain.shape, BF16),
        pltpu.VMEM(kedge.shape, BF16),
        pltpu.VMEM(kcol.shape, BF16),
        pltpu.SMEM((n, LANES), jnp.int32),
        pltpu.SMEM((n, LANES), jnp.int32),
        pltpu.VMEM((n, 8, LANES), F32),
        pltpu.VMEM((n, 8, LANES), F32),
        pltpu.VMEM((slots, srows, width), BF16),
        pltpu.VMEM((slots, srows, width), BF16),
        pltpu.VMEM((slots, srows, LANES), BF16),
        pltpu.VMEM((slots, 8, width), F32),
        pltpu.VMEM((slots, 8, width), F32),
        pltpu.VMEM((slots, srows, width), BF16),
        pltpu.VMEM((band, padded), BF16),
        pltpu.VMEM((2, EDGE, padded), BF16),
        pltpu.VMEM((3, band, padded), BF16),
        pltpu.VMEM((width // LANES, 9 * LANES, 2 * LANES), BF16),
        pltpu.VMEM((band, 2 * LANES), F32),
        pltpu.VMEM((strips, srows, width), BF16),
        pltpu.VMEM((2, n * (span - srows // 2), width // 2 + LANES), BF16),
        pltpu.VMEM((n * srows // 2, width), BF16),
        pltpu.VMEM((n * span, width), BF16),
        pltpu.VMEM((band, n * span), BF16),
        dma((10,)),
        dma((n,)), dma((n,)), dma((n,)), dma((n,)), dma((slots,)), dma((slots,)),
        dma((8,)), dma((8,)),
        dma((3, n)), dma((3, n)),
    ]
    difference, stack = pl.pallas_call(
        functools.partial(kernel, capacity=capacity),
        out_shape=(
            jax.ShapeDtypeStruct((band, width), F32),
            jax.ShapeDtypeStruct((band, width), F32),
        ),
        in_specs=[hbm_spec] * 10,
        out_specs=(pl.BlockSpec(memory_space=pltpu.VMEM),) * 2,
        scratch_shapes=scratch,
        compiler_params=pltpu.CompilerParams(
            collective_id=0, has_side_effects=True, vmem_limit_bytes=40 * 1024 * 1024
        ),
    )(
        pltpu.with_memory_space_constraint(science[0], pltpu.HBM),
        pltpu.with_memory_space_constraint(template.reshape(strips, srows, width), pltpu.HBM),
        pltpu.with_memory_space_constraint(owners.reshape(1, strips), pltpu.HBM),
        pltpu.with_memory_space_constraint(patch_strip.reshape(1, strips), pltpu.HBM),
        pltpu.with_memory_space_constraint(shifts.reshape(2, strips), pltpu.HBM),
        pltpu.with_memory_space_constraint(fractions.reshape(2, strips), pltpu.HBM),
        pltpu.with_memory_space_constraint(coefs.transpose(1, 0, 2), pltpu.HBM),
        pltpu.with_memory_space_constraint(jnp.asarray(kmain), pltpu.HBM),
        pltpu.with_memory_space_constraint(jnp.asarray(kedge), pltpu.HBM),
        pltpu.with_memory_space_constraint(jnp.asarray(kcol), pltpu.HBM),
    )
    difference, stack = pl.pallas_call(
        keep,
        out_shape=(
            jax.ShapeDtypeStruct((band, width), F32),
            jax.ShapeDtypeStruct((band, width), F32),
        ),
        in_specs=[pl.BlockSpec(memory_space=pl.ANY)] * 2,
        out_specs=(hbm_spec, hbm_spec),
        scratch_shapes=[dma((2,))],
    )(
        pltpu.with_memory_space_constraint(difference, pltpu.VMEM),
        pltpu.with_memory_space_constraint(stack, pltpu.VMEM),
    )
    return difference[None], stack.reshape(template.shape)


def solution(mesh):
    return jax.shard_map(
        body,
        mesh=mesh,
        in_specs=(
            P(("grp", "ccd"), "row", "amp"),
            P(("grp", "ccd"), "row", "amp", None, None, None),
            P(("grp", "ccd"), "row", "amp", None, None),
            P(("grp", "ccd"), "row", "amp", None),
            P(("grp", "ccd"), "row", "amp", None, None),
            P(("grp", "ccd"), "row", "amp", None, None),
            P(("grp", "ccd"), None, None),
        ),
        out_specs=(
            P(("grp", "ccd"), "row", "amp"),
            P(("grp", "ccd"), "row", "amp", None, None, None),
        ),
        check_vma=False,
    )
```

```python
import functools

import jax
import jax.numpy as jnp
import ml_dtypes
import numpy as np
from jax import lax
from jax.experimental import pallas as pl
from jax.experimental.pallas import tpu as pltpu
from jax.sharding import PartitionSpec as P

RADIUS = 9
EDGE = 16
LANES = 128
TILE = 256
MESH = pl.DeviceIdType.MESH
F32 = jnp.float32
BF16 = jnp.bfloat16


def kernel_table():
    support = np.arange(-RADIUS, RADIUS + 1).astype(np.float32)
    narrow = np.exp(-support * support / np.float32(4.5))
    slope = support * np.exp(-support * support / np.float32(12.5))
    broad = np.exp(-support * support / np.float32(40.5))
    table = np.stack(
        [narrow / np.sum(narrow), slope / np.sum(np.abs(slope)), broad / np.sum(broad)]
    )
    return table.astype(ml_dtypes.bfloat16)


def toeplitz(kernel, out_at, in_at):
    offset = in_at[None, :] - out_at[:, None] + RADIUS
    inside = (offset >= 0) & (offset <= 2 * RADIUS)
    return np.where(inside, kernel[np.clip(offset, 0, 2 * RADIUS)], np.zeros((), kernel.dtype))


def conv_constants(rows):
    table = kernel_table()
    at = np.arange(rows)
    main = np.concatenate([toeplitz(k, at, at) for k in table], axis=0)
    top = np.stack([toeplitz(k, np.arange(EDGE), np.arange(-EDGE, 0)) for k in table])
    bottom = np.stack(
        [toeplitz(k, np.arange(-EDGE, 0), np.arange(EDGE)) for k in table]
    )
    source = np.arange(-EDGE, LANES + EDGE)
    cols = np.stack([toeplitz(k, np.arange(LANES), source).T for k in table])
    return main, np.stack([top, bottom]), cols


def sinc(value):
    angle = np.float32(np.pi) * value
    return jnp.sin(angle) / angle


def taps_of(offset):
    value = sinc(offset) * sinc(offset / 3.0)
    return value.astype(BF16).astype(F32)


def kernel(
    sci_hbm, tmpl_hbm, own_hbm, pat_hbm, shf_hbm, frc_hbm, cof_hbm, kmain_hbm, kedge_hbm, kcol_hbm,
    diff, stack,
    sci, tmpl, own, pat, shf, frc, cof, kmain, kedge, kcol,
    req_out, req_in, strip_at, meta_out, meta_in, send_buf, fetch, warp_op, taps_fwd, taps_bwd, slot_img,
    img, halo_rows, across, col_op, acc, low, back_free, back_late, back_in, back_op,
    load_sem, req_send, req_recv, meta_send, meta_recv, tmpl_send, tmpl_recv,
    halo_send, halo_recv, back_send, back_recv,
    *, capacity,
):
    n = lax.axis_size("ccd")
    rows_n = lax.axis_size("row")
    cols_n = lax.axis_size("amp")
    me = lax.axis_index("ccd")
    my_row = lax.axis_index("row")
    my_col = lax.axis_index("amp")
    strips, srows, width = tmpl.shape
    band = strips * srows
    span = capacity * srows
    slots = n * capacity
    padded = width + 2 * LANES

    if n == 4:
        low_half = me < n // 2
        at_end = (me == 0) | (me == n - 1)
        near = [jnp.where(low_half, 3, 1), jnp.where(at_end, 2, jnp.where(low_half, 1, 3))]
        near.append(6 - near[0] - near[1])
        distant = [jnp.where(me == 0, 3, jnp.where(me == n - 1, 1, 2)), jnp.where(at_end, 2, jnp.where(low_half, 1, 3))]
        distant.append(6 - distant[0] - distant[1])
    else:
        near = distant = list(range(1, n))

    def peer(d):
        return {"ccd": lax.rem(me + d, n)}

    def back_peer(d):
        return {"ccd": lax.rem(me + n - d, n)}

    loads = [
        pltpu.make_async_copy(src, dst, load_sem.at[i])
        for i, (src, dst) in enumerate(
            [(own_hbm, own), (pat_hbm, pat), (shf_hbm, shf), (frc_hbm, frc), (cof_hbm, cof),
             (tmpl_hbm, tmpl), (kmain_hbm, kmain), (kedge_hbm, kedge), (kcol_hbm, kcol), (sci_hbm, sci)]
        )
    ]
    for load in loads:
        load.start()

    other_row = 1 - 2 * my_row
    other_col = 1 - 2 * my_col
    if rows_n == 2:
        steps = [(0, other_col), (other_row, 0), (other_row, other_col)]
    else:
        steps = [(-1, 0), (1, 0), (0, other_col), (-1, other_col), (1, other_col)]

    def when(step):
        if rows_n == 2 or (not isinstance(step[0], int)) or step[0] == 0:
            return lambda run: run()
        return pl.when((my_row + step[0] >= 0) & (my_row + step[0] < rows_n))

    def neighbour(step):
        return {"row": my_row + step[0], "amp": my_col + step[1]}

    barrier = pltpu.get_barrier_semaphore()
    for d in range(1, n):
        pl.semaphore_signal(barrier, inc=1, device_id=peer(d), device_id_type=MESH)
    for step in steps:
        @when(step)
        def _():
            pl.semaphore_signal(barrier, inc=1, device_id=neighbour(step), device_id_type=MESH)

    loads[0].wait()
    loads[1].wait()
    owner = [own[0, q] for q in range(strips)]
    slot_of = []
    for q in range(strips):
        rank = jnp.int32(0)
        for e in range(q):
            alike = owner[e] == owner[q]
            rank = rank + jnp.where(alike & (my_row == 0) if e == 0 else alike, 1, 0)
        if q == 0:
            rank = jnp.where(my_row == 0, rank, capacity - 1)
        if q == strips - 1:
            rank = jnp.where(my_row == 0, capacity - 1, rank)
        away = owner[q] - me
        away = jnp.where(away < 0, away + n, away)
        slot_of.append(jnp.minimum(away * capacity + rank, slots - 1))
    strip_of = []
    wanted = []
    for s in range(slots):
        q_at = jnp.int32(-1)
        for q in range(strips):
            q_at = jnp.where(slot_of[q] == s, q, q_at)
        q_in = jnp.maximum(q_at, 0)
        strip_of.append(q_in)
        strip_at[0, s] = q_in
        wanted.append(jnp.where(q_at < 0, -1, pat[0, q_in]))
    for d in range(1, n):
        for r in range(capacity):
            req_out[d, r] = jnp.maximum(wanted[d * capacity + r], 0)

    if rows_n == 2:
        around = n - 1 + len(steps)
    else:
        ends = jnp.where(my_row == 0, 1, 0) + jnp.where(my_row == rows_n - 1, 1, 0)
        around = n - 1 + len(steps) - 2 * ends
    pl.semaphore_wait(barrier, around)

    def request(d):
        return pltpu.make_async_remote_copy(
            src_ref=req_out.at[d], dst_ref=req_in.at[d], send_sem=req_send.at[d], recv_sem=req_recv.at[d],
            device_id=peer(d), device_id_type=MESH)

    for d in range(1, n):
        request(d).start()

    loads[5].wait()
    for r in range(capacity):
        fetch[r] = tmpl[jnp.maximum(wanted[r], 0)]

    def reply(d, r):
        s = d * capacity + r
        return pltpu.make_async_remote_copy(
            src_ref=send_buf.at[s], dst_ref=fetch.at[s], send_sem=tmpl_send.at[s], recv_sem=tmpl_recv.at[s],
            device_id=back_peer(d), device_id_type=MESH)

    for d in near:
        request(d).wait_recv()
        for r in range(capacity):
            send_buf[d * capacity + r] = tmpl[req_in[d, r]]
        reply(d, 0).start()
    for r in range(1, capacity):
        for d in near:
            reply(d, r).start()

    lane = lax.broadcasted_iota(jnp.int32, (8, LANES), 1)
    sub = lax.broadcasted_iota(jnp.int32, (8, LANES), 0)
    tap = (sub - 2).astype(F32)

    def meta(d):
        return pltpu.make_async_remote_copy(
            src_ref=meta_out.at[d], dst_ref=meta_in.at[d], send_sem=meta_send.at[d], recv_sem=meta_recv.at[d],
            device_id=peer(d), device_id_type=MESH)

    for i in range(2, 4):
        loads[i].wait()

    def slot_table(s):
        taps = taps_of(tap - frc[0, strip_of[s]])
        return taps, shf[0, strip_of[s]]

    def meta_table(d, rank):
        frac = jnp.full((8, LANES), 0.5, F32)
        shift = jnp.zeros((8, LANES), F32)
        which = jnp.full((8, LANES), -1.0, F32)
        for r in range(capacity):
            s = d * capacity + r
            frac = jnp.where(rank == r, frc[0, strip_of[s]], frac)
            shift = jnp.where(rank == r, shf[0, strip_of[s]].astype(F32), shift)
            which = jnp.where(rank == r, wanted[s].astype(F32), which)
        taps = taps_of(tap - frac)
        return jnp.where(sub == 6, shift, jnp.where(sub == 7, which, taps))

    part_rows = srows // 2
    for d in list(range(1, n)) + [0]:
        meta_out[d] = meta_table(d, lax.rem(lane // srows, capacity))
        if d:
            meta(d).start()

    row_at = lax.broadcasted_iota(jnp.int32, (srows, LANES), 0)
    lane_at = lax.broadcasted_iota(jnp.int32, (srows, LANES), 1)

    def place(table, offset):
        total = jnp.zeros((srows, LANES), F32)
        for t in range(6):
            total = jnp.where(offset == t - 2, table[t:t + 1, :], total)
        return total

    for s in range(slots):
        taps, shift = slot_table(s)
        warp_op[s] = place(taps, lane_at - row_at - shift).astype(BF16)

    col_at = lax.broadcasted_iota(jnp.int32, (8, width), 1)
    tap_at = lax.broadcasted_iota(jnp.int32, (8, width), 0) - 2
    for s in range(slots):
        taps = taps_of(tap - frc[1, strip_of[s]])
        wide = jnp.concatenate([taps] * (width // LANES), axis=1)
        moved = tap_at + shf[1, strip_of[s]]
        ahead, behind = col_at + moved, col_at - moved
        taps_fwd[s] = jnp.where((ahead >= 0) & (ahead < width), wide, 0.0)
        taps_bwd[s] = jnp.where((behind >= 0) & (behind < width), wide, 0.0)

    for i in (4, 6, 7, 8):
        loads[i].wait()
    tiles = width // LANES
    window = 3 * LANES
    first = LANES - EDGE
    last = 2 * LANES + EDGE
    place_x = lax.broadcasted_iota(jnp.int32, (1, LANES), 1).astype(F32) + (my_col * width).astype(F32)
    for j in range(tiles):
        for a in range(3):
            col_op[j, a * window:a * window + first, :] = jnp.zeros((first, 2 * LANES), BF16)
            col_op[j, a * window + last:(a + 1) * window, :] = jnp.zeros((window - last, 2 * LANES), BF16)
    chunk = 80
    for a in range(3):
        @pl.loop(0, (last - first) // chunk)
        def _(i):
            at = pl.ds(pl.multiple_of(i * chunk, 16), chunk)
            base = [kcol[b, at, :].astype(F32) for b in range(3)]
            fold = [
                cof[j, 0, 3 * a] * base[0] + cof[j, 0, 3 * a + 1] * base[1] + cof[j, 0, 3 * a + 2] * base[2]
                for j in range(3)
            ]
            to = pl.ds(pl.multiple_of(a * window + first + i * chunk, 16), chunk)
            for j in range(tiles):
                px = (place_x + (j * LANES + 0.5)) / (width * cols_n) * 2.0 - 1.0
                col_op[j, to, 0:LANES] = (fold[0] + px * fold[1]).astype(BF16)
                col_op[j, to, LANES:] = fold[2].astype(BF16)

    if rows_n == 2:
        halves_at = [pl.multiple_of(part_rows * my_row, part_rows), pl.multiple_of(part_rows * (1 - my_row), part_rows)]
    else:
        halves_at = [0, part_rows]
    late = part_rows
    free = span - late
    group = LANES // span

    right = LANES + width
    col_in = pl.multiple_of(jnp.where(my_col == 0, right, 0), LANES)
    col_out = pl.multiple_of(jnp.where(my_col == 0, 0, right), LANES)
    img[:, pl.ds(col_out, LANES)] = jnp.zeros((band, LANES), BF16)
    halo_rows[:, :, pl.ds(col_out, LANES)] = jnp.zeros((2, EDGE, LANES), BF16)
    if rows_n > 2:
        @pl.when(my_row == 0)
        def _():
            halo_rows[0] = jnp.zeros((EDGE, padded), BF16)

        @pl.when(my_row == rows_n - 1)
        def _():
            halo_rows[1] = jnp.zeros((EDGE, padded), BF16)
    for a in range(3):
        across[a, :, pl.ds(col_out, LANES)] = jnp.zeros((band, LANES), BF16)

    for r in range(capacity):
        for d in range(n):
            s = d * capacity + r
            if d:
                reply(d, r).wait_recv()
            value = jnp.dot(warp_op[s, :, :srows], fetch[s], preferred_element_type=F32).astype(BF16)
            move = shf[1, strip_of[s]]
            total = jnp.zeros((srows, width), F32)
            for t in range(6):
                moved = pltpu.roll(value, width - (move + (t - 2)), 1).astype(F32)
                total = total + taps_fwd[s, t:t + 1, :] * moved
            slot_img[s] = total.astype(BF16)
    for q in range(strips):
        img[q * srows:(q + 1) * srows, LANES:right] = slot_img[slot_of[q]]

    def halo(i):
        step = steps[i]
        if isinstance(step[1], int):
            cols_src = cols_dst = pl.ds(LANES, width)
        else:
            cols_src = pl.ds(pl.multiple_of(jnp.where(my_col == 0, right - LANES, LANES), LANES), LANES)
            cols_dst = pl.ds(col_out, LANES)
        if isinstance(step[0], int) and step[0] == 0:
            src, dst = img.at[:, cols_src], img.at[:, cols_dst]
        elif isinstance(step[0], int):
            top = band - EDGE if step[0] > 0 else 0
            src = img.at[pl.ds(top, EDGE), cols_src]
            dst = halo_rows.at[0 if step[0] > 0 else 1, :, cols_dst]
        else:
            top = pl.multiple_of(jnp.where(my_row == 0, band - EDGE, 0), EDGE)
            src = img.at[pl.ds(top, EDGE), cols_src]
            dst = halo_rows.at[my_row, :, cols_dst]
        return pltpu.make_async_remote_copy(
            src_ref=src, dst_ref=dst, send_sem=halo_send.at[i], recv_sem=halo_recv.at[i],
            device_id=neighbour(step), device_id_type=MESH)

    for i, step in enumerate(steps):
        @when(step)
        def _(i=i):
            halo(i).start()

    def received(step):
        if isinstance(step[0], int):
            return (-step[0], step[1])
        return step

    def await_halo(at):
        @when(received(steps[at]))
        def _():
            halo(at).wait_recv()

    def across_of(col, count):
        for a in range(3):
            total = jnp.dot(kmain[a * band:(a + 1) * band, :], img[:, pl.ds(col, count)], preferred_element_type=F32)
            across[a, :, pl.ds(col, count)] = total.astype(BF16)

    if rows_n == 2:
        edges = [(1 - my_row, pl.multiple_of(jnp.where(my_row == 0, band - EDGE, 0), EDGE))]
    else:
        edges = [(0, 0), (1, band - EDGE)]

    def edge_rows():
        for a in range(3):
            for side, top in edges:
                near = kmain[pl.ds(pl.multiple_of(a * band + top, EDGE), EDGE), :]
                total = jnp.dot(near, img[...], preferred_element_type=F32)
                total = total + jnp.dot(kedge[side, a], halo_rows[side], preferred_element_type=F32)
                across[a, pl.ds(top, EDGE), :] = total.astype(BF16)

    def subtract(turn, top, rows):
        tile = my_col * (tiles - 1) + turn * (1 - 2 * my_col)
        here = pl.ds(top, rows)
        at = pl.ds(pl.multiple_of(tile * LANES, LANES), window)
        lhs = jnp.concatenate([across[a, here, at] for a in range(3)], axis=1)
        acc[0:rows, :] = jnp.dot(lhs, col_op[tile], preferred_element_type=F32)
        at = pl.ds(pl.multiple_of(tile * LANES, LANES), LANES)
        step = min(rows, srows)
        local = lax.broadcasted_iota(jnp.int32, (step, LANES), 0)
        for q in range(rows // step):
            y = local + (my_row * band + top + q * step)
            py = (y.astype(F32) + 0.5) / (band * rows_n) * 2.0 - 1.0
            part = slice(q * step, (q + 1) * step)
            to = pl.ds(pl.multiple_of(top + q * step, step), step)
            value = sci[to, at] - (acc[part, 0:LANES] + py * acc[part, LANES:])
            diff[to, at] = value
            strip = top // srows + q
            low[strip, pl.ds(pl.multiple_of(top - top // srows * srows, step), step), at] = value.astype(BF16)

    piece_cols = width // 2
    region = piece_cols + LANES

    def piece_at(piece):
        inner = my_col if piece == 0 else 1 - my_col
        return pl.multiple_of(inner * piece_cols, LANES), pl.multiple_of(inner * LANES, LANES)

    def give(d, piece):
        if piece == 2:
            src = back_late.at[pl.ds(pl.multiple_of(d * late, late), late)]
            dst = back_in.at[pl.ds(pl.multiple_of(d * span + free, late), late)]
        else:
            at, offset = piece_at(piece)
            src = back_free.at[piece, pl.ds(pl.multiple_of(d * free, late), free), pl.ds(offset, piece_cols)]
            dst = back_in.at[pl.ds(pl.multiple_of(d * span, late), free), pl.ds(at, piece_cols)]
        return pltpu.make_async_remote_copy(
            src_ref=src, dst_ref=dst, send_sem=back_send.at[piece, d], recv_sem=back_recv.at[piece, d],
            device_id=peer(d), device_id_type=MESH)

    def column_sum(s, top, rows, source, cols):
        value = low[strip_at[0, s], pl.ds(top, rows), source]
        move = shf[1, strip_at[0, s]]
        total = jnp.zeros((rows, cols), F32)
        for t in range(6):
            moved = pltpu.roll(value, cols + (move + (t - 2)), 1).astype(F32)
            total = total + taps_bwd[s, t:t + 1, source] * moved
        return total.astype(BF16)

    def columns_back(piece):
        if piece < 2:
            at, offset = piece_at(piece)
            source = pl.ds(pl.multiple_of(at - offset, LANES), region)
        for d in distant + [0]:
            if piece == 2:
                back_late[pl.ds(pl.multiple_of(d * late, late), late), :] = column_sum(
                    (d + 1) * capacity - 1, halves_at[1], late, pl.ds(0, width), width)
            else:
                for r in range(capacity):
                    rows = srows if r < capacity - 1 else srows - late
                    top = 0 if r < capacity - 1 else halves_at[0]
                    to = pl.ds(pl.multiple_of(d * free + r * srows, late), rows)
                    back_free[piece, to, :] = column_sum(d * capacity + r, top, rows, source, region)
            if not (isinstance(d, int) and d == 0):
                give(d, piece).start()
        if piece == 2:
            back_in[free:span, :] = back_late[0:late, :]
        else:
            back_in[0:free, pl.ds(at, piece_cols)] = back_free[piece, 0:free, pl.ds(offset, piece_cols)]

    amp_at = [i for i, step in enumerate(steps) if isinstance(step[0], int) and step[0] == 0]
    row_at_steps = [i for i in range(len(steps)) if i not in amp_at]

    def finish_edges():
        for i in row_at_steps:
            await_halo(i)
        edge_rows()

    loads[9].wait()
    for c in range(width // TILE):
        across_of(pl.multiple_of(LANES + (c + (1 - 2 * c) * my_col) * TILE, LANES), TILE)
    if rows_n > 2:
        for i in amp_at:
            await_halo(i)
        across_of(col_in, LANES)
        finish_edges()
    for turn in range(tiles - 1):
        subtract(turn, 0, band)
    columns_back(0)
    if rows_n == 2:
        for i in amp_at:
            await_halo(i)
        across_of(col_in, LANES)
    subtract(tiles - 1, 0, band)
    columns_back(1)
    if rows_n == 2:
        finish_edges()
        for turn in range(tiles):
            subtract(turn, edges[0][1], EDGE)
    columns_back(2)

    span_at = lax.rem(lane_at, span)
    late_at = lax.rem(span_at, part_rows) + jnp.where(span_at < free, halves_at[0], halves_at[1])
    from_row = jnp.where(span_at < span - srows, lax.rem(span_at, srows), late_at)
    for g in range(n // group):
        for e in range(group):
            d = g * group + e
            if d:
                meta(d).wait_recv()
            came = meta_in[d] if d else meta_out[0]
            table = came if e == 0 else jnp.where(lane // span == e, came, table)
        shift = table[6:7, :].astype(jnp.int32)
        which = table[7:8, :].astype(jnp.int32)
        operator = place(table, row_at - from_row - shift)
        for p in range(strips):
            back_op[p * srows:(p + 1) * srows, g * LANES:(g + 1) * LANES] = jnp.where(which == p, operator, 0.0).astype(BF16)

    for piece in range(3):
        for d in range(1, n):
            give(d, piece).wait_recv()
    stack[...] = jnp.dot(back_op[...], back_in[...], preferred_element_type=F32)

    for d in range(1, n):
        request(d).wait_send()
        for r in range(capacity):
            reply(d, r).wait_send()
        meta(d).wait_send()
        for piece in range(3):
            give(d, piece).wait_send()
    for i, step in enumerate(steps):
        @when(step)
        def _(i=i):
            halo(i).wait_send()


def keep(diff, stack, diff_out, stack_out, sem):
    copies = [
        pltpu.make_async_copy(diff, diff_out, sem.at[0]),
        pltpu.make_async_copy(stack, stack_out, sem.at[1]),
    ]
    for copy in copies:
        copy.start()
    for copy in copies:
        copy.wait()


def body(science, template, owners, patch_strip, shifts, fractions, coefs):
    n = lax.axis_size("ccd")
    band, width = science.shape[1:]
    strips, srows = template.shape[3:5]
    capacity = max(2, strips // n)
    slots = n * capacity
    span = capacity * srows
    padded = width + 2 * LANES
    kmain, kedge, kcol = conv_constants(band)
    hbm_spec = pl.BlockSpec(memory_space=pltpu.HBM)
    dma = pltpu.SemaphoreType.DMA
    scratch = [
        pltpu.VMEM((band, width), F32),
        pltpu.VMEM((strips, srows, width), BF16),
        pltpu.SMEM((1, strips), jnp.int32),
        pltpu.SMEM((1, strips), jnp.int32),
        pltpu.SMEM((2, strips), jnp.int32),
        pltpu.SMEM((2, strips), F32),
        pltpu.SMEM((3, 1, 9), F32),
        pltpu.VMEM(kmain.shape, BF16),
        pltpu.VMEM(kedge.shape, BF16),
        pltpu.VMEM(kcol.shape, BF16),
        pltpu.SMEM((n, LANES), jnp.int32),
        pltpu.SMEM((n, LANES), jnp.int32),
        pltpu.SMEM((1, slots), jnp.int32),
        pltpu.VMEM((n, 8, LANES), F32),
        pltpu.VMEM((n, 8, LANES), F32),
        pltpu.VMEM((slots, srows, width), BF16),
        pltpu.VMEM((slots, srows, width), BF16),
        pltpu.VMEM((slots, srows, LANES), BF16),
        pltpu.VMEM((slots, 8, width), F32),
        pltpu.VMEM((slots, 8, width), F32),
        pltpu.VMEM((slots, srows, width), BF16),
        pltpu.VMEM((band, padded), BF16),
        pltpu.VMEM((2, EDGE, padded), BF16),
        pltpu.VMEM((3, band, padded), BF16),
        pltpu.VMEM((width // LANES, 9 * LANES, 2 * LANES), BF16),
        pltpu.VMEM((band, 2 * LANES), F32),
        pltpu.VMEM((strips, srows, width), BF16),
        pltpu.VMEM((2, n * (span - srows // 2), width // 2 + LANES), BF16),
        pltpu.VMEM((n * srows // 2, width), BF16),
        pltpu.VMEM((n * span, width), BF16),
        pltpu.VMEM((band, n * span), BF16),
        dma((10,)),
        dma((n,)), dma((n,)), dma((n,)), dma((n,)), dma((slots,)), dma((slots,)),
        dma((8,)), dma((8,)),
        dma((3, n)), dma((3, n)),
    ]
    difference, stack = pl.pallas_call(
        functools.partial(kernel, capacity=capacity),
        out_shape=(
            jax.ShapeDtypeStruct((band, width), F32),
            jax.ShapeDtypeStruct((band, width), F32),
        ),
        in_specs=[hbm_spec] * 10,
        out_specs=(pl.BlockSpec(memory_space=pltpu.VMEM),) * 2,
        scratch_shapes=scratch,
        compiler_params=pltpu.CompilerParams(
            collective_id=0, has_side_effects=True, vmem_limit_bytes=40 * 1024 * 1024
        ),
    )(
        pltpu.with_memory_space_constraint(science[0], pltpu.HBM),
        pltpu.with_memory_space_constraint(template.reshape(strips, srows, width), pltpu.HBM),
        pltpu.with_memory_space_constraint(owners.reshape(1, strips), pltpu.HBM),
        pltpu.with_memory_space_constraint(patch_strip.reshape(1, strips), pltpu.HBM),
        pltpu.with_memory_space_constraint(shifts.reshape(2, strips), pltpu.HBM),
        pltpu.with_memory_space_constraint(fractions.reshape(2, strips), pltpu.HBM),
        pltpu.with_memory_space_constraint(coefs.transpose(1, 0, 2), pltpu.HBM),
        pltpu.with_memory_space_constraint(jnp.asarray(kmain), pltpu.HBM),
        pltpu.with_memory_space_constraint(jnp.asarray(kedge), pltpu.HBM),
        pltpu.with_memory_space_constraint(jnp.asarray(kcol), pltpu.HBM),
    )
    difference, stack = pl.pallas_call(
        keep,
        out_shape=(
            jax.ShapeDtypeStruct((band, width), F32),
            jax.ShapeDtypeStruct((band, width), F32),
        ),
        in_specs=[pl.BlockSpec(memory_space=pl.ANY)] * 2,
        out_specs=(hbm_spec, hbm_spec),
        scratch_shapes=[dma((2,))],
    )(
        pltpu.with_memory_space_constraint(difference, pltpu.VMEM),
        pltpu.with_memory_space_constraint(stack, pltpu.VMEM),
    )
    return difference[None], stack.reshape(template.shape)


def solution(mesh):
    return jax.shard_map(
        body,
        mesh=mesh,
        in_specs=(
            P(("grp", "ccd"), "row", "amp"),
            P(("grp", "ccd"), "row", "amp", None, None, None),
            P(("grp", "ccd"), "row", "amp", None, None),
            P(("grp", "ccd"), "row", "amp", None),
            P(("grp", "ccd"), "row", "amp", None, None),
            P(("grp", "ccd"), "row", "amp", None, None),
            P(("grp", "ccd"), None, None),
        ),
        out_specs=(
            P(("grp", "ccd"), "row", "amp"),
            P(("grp", "ccd"), "row", "amp", None, None, None),
        ),
        check_vma=False,
    )
```

```python
import functools

import jax
import jax.numpy as jnp
import ml_dtypes
import numpy as np
from jax import lax
from jax.experimental import pallas as pl
from jax.experimental.pallas import tpu as pltpu
from jax.sharding import PartitionSpec as P

RADIUS = 9
EDGE = 16
LANES = 128
TILE = 256
MESH = pl.DeviceIdType.MESH
F32 = jnp.float32
BF16 = jnp.bfloat16


def kernel_table():
    support = np.arange(-RADIUS, RADIUS + 1).astype(np.float32)
    narrow = np.exp(-support * support / np.float32(4.5))
    slope = support * np.exp(-support * support / np.float32(12.5))
    broad = np.exp(-support * support / np.float32(40.5))
    table = np.stack(
        [narrow / np.sum(narrow), slope / np.sum(np.abs(slope)), broad / np.sum(broad)]
    )
    return table.astype(ml_dtypes.bfloat16)


def toeplitz(kernel, out_at, in_at):
    offset = in_at[None, :] - out_at[:, None] + RADIUS
    inside = (offset >= 0) & (offset <= 2 * RADIUS)
    return np.where(inside, kernel[np.clip(offset, 0, 2 * RADIUS)], np.zeros((), kernel.dtype))


def conv_constants(rows):
    table = kernel_table()
    at = np.arange(rows)
    main = np.concatenate([toeplitz(k, at, at) for k in table], axis=0)
    top = np.stack([toeplitz(k, np.arange(EDGE), np.arange(-EDGE, 0)) for k in table])
    bottom = np.stack(
        [toeplitz(k, np.arange(-EDGE, 0), np.arange(EDGE)) for k in table]
    )
    source = np.arange(-EDGE, LANES + EDGE)
    cols = np.stack([toeplitz(k, np.arange(LANES), source).T for k in table])
    return main, np.stack([top, bottom]), cols


def sinc(value):
    angle = np.float32(np.pi) * value
    return jnp.sin(angle) / angle


def taps_of(offset):
    value = sinc(offset) * sinc(offset / 3.0)
    return value.astype(BF16).astype(F32)


def kernel(
    sci_hbm, tmpl_hbm, own_hbm, pat_hbm, shf_hbm, frc_hbm, cof_hbm, kmain_hbm, kedge_hbm, kcol_hbm,
    diff, back_in, back_op,
    sci, tmpl, own, pat, shf, frc, cof, kmain, kedge, kcol,
    req_out, req_in, strip_at, meta_out, meta_in, send_buf, fetch, warp_op, taps_fwd, taps_bwd, slot_img,
    img, halo_rows, across, col_op, acc, low, back_free, back_late,
    load_sem, req_send, req_recv, meta_send, meta_recv, tmpl_send, tmpl_recv,
    halo_send, halo_recv, back_send, back_recv,
    *, capacity,
):
    n = lax.axis_size("ccd")
    rows_n = lax.axis_size("row")
    cols_n = lax.axis_size("amp")
    me = lax.axis_index("ccd")
    my_row = lax.axis_index("row")
    my_col = lax.axis_index("amp")
    strips, srows, width = tmpl.shape
    band = strips * srows
    span = capacity * srows
    slots = n * capacity
    padded = width + 2 * LANES

    if n == 4:
        low_half = me < n // 2
        at_end = (me == 0) | (me == n - 1)
        near = [jnp.where(low_half, 3, 1), jnp.where(at_end, 2, jnp.where(low_half, 1, 3))]
        near.append(6 - near[0] - near[1])
        distant = [jnp.where(me == 0, 3, jnp.where(me == n - 1, 1, 2)), jnp.where(at_end, 2, jnp.where(low_half, 1, 3))]
        distant.append(6 - distant[0] - distant[1])
    else:
        near = distant = list(range(1, n))

    def peer(d):
        return {"ccd": lax.rem(me + d, n)}

    def back_peer(d):
        return {"ccd": lax.rem(me + n - d, n)}

    other_row = 1 - 2 * my_row
    other_col = 1 - 2 * my_col
    if rows_n == 2:
        steps = [(0, other_col), (other_row, 0), (other_row, other_col)]
    else:
        steps = [(-1, 0), (1, 0), (0, other_col), (-1, other_col), (1, other_col)]

    def when(step):
        if rows_n == 2 or (not isinstance(step[0], int)) or step[0] == 0:
            return lambda run: run()
        return pl.when((my_row + step[0] >= 0) & (my_row + step[0] < rows_n))

    def neighbour(step):
        return {"row": my_row + step[0], "amp": my_col + step[1]}

    barrier = pltpu.get_barrier_semaphore()
    for d in range(1, n):
        pl.semaphore_signal(barrier, inc=1, device_id=peer(d), device_id_type=MESH)
    for step in steps:
        @when(step)
        def _():
            pl.semaphore_signal(barrier, inc=1, device_id=neighbour(step), device_id_type=MESH)

    loads = [
        pltpu.make_async_copy(src, dst, load_sem.at[i])
        for i, (src, dst) in enumerate(
            [(own_hbm, own), (pat_hbm, pat), (shf_hbm, shf), (frc_hbm, frc), (cof_hbm, cof),
             (tmpl_hbm, tmpl), (kmain_hbm, kmain), (kedge_hbm, kedge), (kcol_hbm, kcol), (sci_hbm, sci)]
        )
    ]
    for load in loads:
        load.start()

    loads[0].wait()
    loads[1].wait()
    owner = [own[0, q] for q in range(strips)]
    slot_of = []
    for q in range(strips):
        rank = jnp.int32(0)
        for e in range(q):
            alike = owner[e] == owner[q]
            rank = rank + jnp.where(alike & (my_row == 0) if e == 0 else alike, 1, 0)
        if q == 0:
            rank = jnp.where(my_row == 0, rank, capacity - 1)
        if q == strips - 1:
            rank = jnp.where(my_row == 0, capacity - 1, rank)
        away = owner[q] - me
        away = jnp.where(away < 0, away + n, away)
        slot_of.append(jnp.minimum(away * capacity + rank, slots - 1))
    strip_of = []
    wanted = []
    for s in range(slots):
        q_at = jnp.int32(-1)
        for q in range(strips):
            q_at = jnp.where(slot_of[q] == s, q, q_at)
        q_in = jnp.maximum(q_at, 0)
        strip_of.append(q_in)
        strip_at[0, s] = q_in
        wanted.append(jnp.where(q_at < 0, -1, pat[0, q_in]))
    for d in range(1, n):
        for r in range(capacity):
            req_out[d, r] = jnp.maximum(wanted[d * capacity + r], 0)

    if rows_n == 2:
        around = n - 1 + len(steps)
    else:
        ends = jnp.where(my_row == 0, 1, 0) + jnp.where(my_row == rows_n - 1, 1, 0)
        around = n - 1 + len(steps) - 2 * ends
    pl.semaphore_wait(barrier, around)

    def request(d):
        return pltpu.make_async_remote_copy(
            src_ref=req_out.at[d], dst_ref=req_in.at[d], send_sem=req_send.at[d], recv_sem=req_recv.at[d],
            device_id=peer(d), device_id_type=MESH)

    for d in range(1, n):
        request(d).start()

    loads[5].wait()
    for r in range(capacity):
        fetch[r] = tmpl[jnp.maximum(wanted[r], 0)]

    def reply(d, r):
        s = d * capacity + r
        return pltpu.make_async_remote_copy(
            src_ref=send_buf.at[s], dst_ref=fetch.at[s], send_sem=tmpl_send.at[s], recv_sem=tmpl_recv.at[s],
            device_id=back_peer(d), device_id_type=MESH)

    for d in near:
        request(d).wait_recv()
        for r in range(capacity):
            send_buf[d * capacity + r] = tmpl[req_in[d, r]]
        reply(d, 0).start()
    for r in range(1, capacity):
        for d in near:
            reply(d, r).start()

    lane = lax.broadcasted_iota(jnp.int32, (8, LANES), 1)
    sub = lax.broadcasted_iota(jnp.int32, (8, LANES), 0)
    tap = (sub - 2).astype(F32)

    def meta(d):
        return pltpu.make_async_remote_copy(
            src_ref=meta_out.at[d], dst_ref=meta_in.at[d], send_sem=meta_send.at[d], recv_sem=meta_recv.at[d],
            device_id=peer(d), device_id_type=MESH)

    for i in range(2, 4):
        loads[i].wait()

    def slot_table(s):
        taps = taps_of(tap - frc[0, strip_of[s]])
        return taps, shf[0, strip_of[s]]

    def meta_table(d, rank):
        frac = jnp.full((8, LANES), 0.5, F32)
        shift = jnp.zeros((8, LANES), F32)
        which = jnp.full((8, LANES), -1.0, F32)
        for r in range(capacity):
            s = d * capacity + r
            frac = jnp.where(rank == r, frc[0, strip_of[s]], frac)
            shift = jnp.where(rank == r, shf[0, strip_of[s]].astype(F32), shift)
            which = jnp.where(rank == r, wanted[s].astype(F32), which)
        taps = taps_of(tap - frac)
        return jnp.where(sub == 6, shift, jnp.where(sub == 7, which, taps))

    part_rows = srows // 2
    for d in list(range(1, n)) + [0]:
        meta_out[d] = meta_table(d, lax.rem(lane // srows, capacity))
        if d:
            meta(d).start()

    row_at = lax.broadcasted_iota(jnp.int32, (srows, LANES), 0)
    lane_at = lax.broadcasted_iota(jnp.int32, (srows, LANES), 1)

    def place(table, offset):
        total = jnp.zeros((srows, LANES), F32)
        for t in range(6):
            total = jnp.where(offset == t - 2, table[t:t + 1, :], total)
        return total

    for s in range(slots):
        taps, shift = slot_table(s)
        warp_op[s] = place(taps, lane_at - row_at - shift).astype(BF16)

    col_at = lax.broadcasted_iota(jnp.int32, (8, width), 1)
    tap_at = lax.broadcasted_iota(jnp.int32, (8, width), 0) - 2
    for s in range(slots):
        taps = taps_of(tap - frc[1, strip_of[s]])
        wide = jnp.concatenate([taps] * (width // LANES), axis=1)
        moved = tap_at + shf[1, strip_of[s]]
        ahead, behind = col_at + moved, col_at - moved
        taps_fwd[s] = jnp.where((ahead >= 0) & (ahead < width), wide, 0.0)
        taps_bwd[s] = jnp.where((behind >= 0) & (behind < width), wide, 0.0)

    for i in (4, 6, 7, 8):
        loads[i].wait()
    tiles = width // LANES
    window = 3 * LANES
    first = LANES - EDGE
    last = 2 * LANES + EDGE
    place_x = lax.broadcasted_iota(jnp.int32, (1, LANES), 1).astype(F32) + (my_col * width).astype(F32)
    for j in range(tiles):
        for a in range(3):
            col_op[j, a * window:a * window + first, :] = jnp.zeros((first, 2 * LANES), BF16)
            col_op[j, a * window + last:(a + 1) * window, :] = jnp.zeros((window - last, 2 * LANES), BF16)
    chunk = 80
    for a in range(3):
        @pl.loop(0, (last - first) // chunk)
        def _(i):
            at = pl.ds(pl.multiple_of(i * chunk, 16), chunk)
            base = [kcol[b, at, :].astype(F32) for b in range(3)]
            fold = [
                cof[j, 0, 3 * a] * base[0] + cof[j, 0, 3 * a + 1] * base[1] + cof[j, 0, 3 * a + 2] * base[2]
                for j in range(3)
            ]
            to = pl.ds(pl.multiple_of(a * window + first + i * chunk, 16), chunk)
            for j in range(tiles):
                px = (place_x + (j * LANES + 0.5)) / (width * cols_n) * 2.0 - 1.0
                col_op[j, to, 0:LANES] = (fold[0] + px * fold[1]).astype(BF16)
                col_op[j, to, LANES:] = fold[2].astype(BF16)

    if rows_n == 2:
        halves_at = [pl.multiple_of(part_rows * my_row, part_rows), pl.multiple_of(part_rows * (1 - my_row), part_rows)]
    else:
        halves_at = [0, part_rows]
    late = part_rows
    free = span - late
    group = LANES // span

    right = LANES + width
    col_in = pl.multiple_of(jnp.where(my_col == 0, right, 0), LANES)
    col_out = pl.multiple_of(jnp.where(my_col == 0, 0, right), LANES)
    img[:, pl.ds(col_out, LANES)] = jnp.zeros((band, LANES), BF16)
    halo_rows[:, :, pl.ds(col_out, LANES)] = jnp.zeros((2, EDGE, LANES), BF16)
    if rows_n > 2:
        @pl.when(my_row == 0)
        def _():
            halo_rows[0] = jnp.zeros((EDGE, padded), BF16)

        @pl.when(my_row == rows_n - 1)
        def _():
            halo_rows[1] = jnp.zeros((EDGE, padded), BF16)
    for a in range(3):
        across[a, :, pl.ds(col_out, LANES)] = jnp.zeros((band, LANES), BF16)

    for r in range(capacity):
        for d in range(n):
            s = d * capacity + r
            if d:
                reply(d, r).wait_recv()
            value = jnp.dot(warp_op[s, :, :srows], fetch[s], preferred_element_type=F32).astype(BF16)
            move = shf[1, strip_of[s]]
            total = jnp.zeros((srows, width), F32)
            for t in range(6):
                moved = pltpu.roll(value, width - (move + (t - 2)), 1).astype(F32)
                total = total + taps_fwd[s, t:t + 1, :] * moved
            slot_img[s] = total.astype(BF16)
    for q in range(strips):
        img[q * srows:(q + 1) * srows, LANES:right] = slot_img[slot_of[q]]

    def halo(i):
        step = steps[i]
        if isinstance(step[1], int):
            cols_src = cols_dst = pl.ds(LANES, width)
        else:
            cols_src = pl.ds(pl.multiple_of(jnp.where(my_col == 0, right - LANES, LANES), LANES), LANES)
            cols_dst = pl.ds(col_out, LANES)
        if isinstance(step[0], int) and step[0] == 0:
            src, dst = img.at[:, cols_src], img.at[:, cols_dst]
        elif isinstance(step[0], int):
            top = band - EDGE if step[0] > 0 else 0
            src = img.at[pl.ds(top, EDGE), cols_src]
            dst = halo_rows.at[0 if step[0] > 0 else 1, :, cols_dst]
        else:
            top = pl.multiple_of(jnp.where(my_row == 0, band - EDGE, 0), EDGE)
            src = img.at[pl.ds(top, EDGE), cols_src]
            dst = halo_rows.at[my_row, :, cols_dst]
        return pltpu.make_async_remote_copy(
            src_ref=src, dst_ref=dst, send_sem=halo_send.at[i], recv_sem=halo_recv.at[i],
            device_id=neighbour(step), device_id_type=MESH)

    for i, step in enumerate(steps):
        @when(step)
        def _(i=i):
            halo(i).start()

    def received(step):
        if isinstance(step[0], int):
            return (-step[0], step[1])
        return step

    def await_halo(at):
        @when(received(steps[at]))
        def _():
            halo(at).wait_recv()

    def across_of(col, count):
        for a in range(3):
            total = jnp.dot(kmain[a * band:(a + 1) * band, :], img[:, pl.ds(col, count)], preferred_element_type=F32)
            across[a, :, pl.ds(col, count)] = total.astype(BF16)

    if rows_n == 2:
        edges = [(1 - my_row, pl.multiple_of(jnp.where(my_row == 0, band - EDGE, 0), EDGE))]
    else:
        edges = [(0, 0), (1, band - EDGE)]

    def edge_rows():
        for a in range(3):
            for side, top in edges:
                near = kmain[pl.ds(pl.multiple_of(a * band + top, EDGE), EDGE), :]
                total = jnp.dot(near, img[...], preferred_element_type=F32)
                total = total + jnp.dot(kedge[side, a], halo_rows[side], preferred_element_type=F32)
                across[a, pl.ds(top, EDGE), :] = total.astype(BF16)

    def subtract(turn, top, rows):
        tile = my_col * (tiles - 1) + turn * (1 - 2 * my_col)
        here = pl.ds(top, rows)
        at = pl.ds(pl.multiple_of(tile * LANES, LANES), window)
        lhs = jnp.concatenate([across[a, here, at] for a in range(3)], axis=1)
        acc[0:rows, :] = jnp.dot(lhs, col_op[tile], preferred_element_type=F32)
        at = pl.ds(pl.multiple_of(tile * LANES, LANES), LANES)
        step = min(rows, srows)
        local = lax.broadcasted_iota(jnp.int32, (step, LANES), 0)
        for q in range(rows // step):
            y = local + (my_row * band + top + q * step)
            py = (y.astype(F32) + 0.5) / (band * rows_n) * 2.0 - 1.0
            part = slice(q * step, (q + 1) * step)
            to = pl.ds(pl.multiple_of(top + q * step, step), step)
            value = sci[to, at] - (acc[part, 0:LANES] + py * acc[part, LANES:])
            diff[to, at] = value
            strip = top // srows + q
            low[strip, pl.ds(pl.multiple_of(top - top // srows * srows, step), step), at] = value.astype(BF16)

    piece_cols = width // 2
    region = piece_cols + LANES

    def piece_at(piece):
        inner = my_col if piece == 0 else 1 - my_col
        return pl.multiple_of(inner * piece_cols, LANES), pl.multiple_of(inner * LANES, LANES)

    def give(d, piece):
        if piece == 2:
            src = back_late.at[pl.ds(pl.multiple_of(d * late, late), late)]
            dst = back_in.at[pl.ds(pl.multiple_of(d * span + free, late), late)]
        else:
            at, offset = piece_at(piece)
            src = back_free.at[piece, pl.ds(pl.multiple_of(d * free, late), free), pl.ds(offset, piece_cols)]
            dst = back_in.at[pl.ds(pl.multiple_of(d * span, late), free), pl.ds(at, piece_cols)]
        return pltpu.make_async_remote_copy(
            src_ref=src, dst_ref=dst, send_sem=back_send.at[piece, d], recv_sem=back_recv.at[piece, d],
            device_id=peer(d), device_id_type=MESH)

    def column_sum(s, top, rows, source, cols):
        value = low[strip_at[0, s], pl.ds(top, rows), source]
        move = shf[1, strip_at[0, s]]
        total = jnp.zeros((rows, cols), F32)
        for t in range(6):
            moved = pltpu.roll(value, cols + (move + (t - 2)), 1).astype(F32)
            total = total + taps_bwd[s, t:t + 1, source] * moved
        return total.astype(BF16)

    def columns_back(piece):
        if piece < 2:
            at, offset = piece_at(piece)
            source = pl.ds(pl.multiple_of(at - offset, LANES), region)
        for d in distant + [0]:
            if piece == 2:
                back_late[pl.ds(pl.multiple_of(d * late, late), late), :] = column_sum(
                    (d + 1) * capacity - 1, halves_at[1], late, pl.ds(0, width), width)
            else:
                for r in range(capacity):
                    rows = srows if r < capacity - 1 else srows - late
                    top = 0 if r < capacity - 1 else halves_at[0]
                    to = pl.ds(pl.multiple_of(d * free + r * srows, late), rows)
                    back_free[piece, to, :] = column_sum(d * capacity + r, top, rows, source, region)
            if not (isinstance(d, int) and d == 0):
                give(d, piece).start()
        if piece == 2:
            back_in[free:span, :] = back_late[0:late, :]
        else:
            back_in[0:free, pl.ds(at, piece_cols)] = back_free[piece, 0:free, pl.ds(offset, piece_cols)]

    amp_at = [i for i, step in enumerate(steps) if isinstance(step[0], int) and step[0] == 0]
    row_at_steps = [i for i in range(len(steps)) if i not in amp_at]

    def finish_edges():
        for i in row_at_steps:
            await_halo(i)
        edge_rows()

    loads[9].wait()
    for c in range(width // TILE):
        across_of(pl.multiple_of(LANES + (c + (1 - 2 * c) * my_col) * TILE, LANES), TILE)
    if rows_n > 2:
        for i in amp_at:
            await_halo(i)
        across_of(col_in, LANES)
        finish_edges()
    for turn in range(tiles - 1):
        subtract(turn, 0, band)
    columns_back(0)
    if rows_n == 2:
        for i in amp_at:
            await_halo(i)
        across_of(col_in, LANES)
    subtract(tiles - 1, 0, band)
    columns_back(1)
    if rows_n == 2:
        finish_edges()
        for turn in range(tiles):
            subtract(turn, edges[0][1], EDGE)
    columns_back(2)

    span_at = lax.rem(lane_at, span)
    late_at = lax.rem(span_at, part_rows) + jnp.where(span_at < free, halves_at[0], halves_at[1])
    from_row = jnp.where(span_at < span - srows, lax.rem(span_at, srows), late_at)
    for g in range(n // group):
        for e in range(group):
            d = g * group + e
            if d:
                meta(d).wait_recv()
            came = meta_in[d] if d else meta_out[0]
            table = came if e == 0 else jnp.where(lane // span == e, came, table)
        shift = table[6:7, :].astype(jnp.int32)
        which = table[7:8, :].astype(jnp.int32)
        operator = place(table, row_at - from_row - shift)
        for p in range(strips):
            back_op[p * srows:(p + 1) * srows, g * LANES:(g + 1) * LANES] = jnp.where(which == p, operator, 0.0).astype(BF16)

    for piece in range(3):
        for d in range(1, n):
            give(d, piece).wait_recv()

    for d in range(1, n):
        request(d).wait_send()
        for r in range(capacity):
            reply(d, r).wait_send()
        meta(d).wait_send()
        for piece in range(3):
            give(d, piece).wait_send()
    for i, step in enumerate(steps):
        @when(step)
        def _(i=i):
            halo(i).wait_send()


def finish(diff, back_in, back_op, diff_out, stack_out, stack, sem):
    copies = [pltpu.make_async_copy(diff, diff_out, sem.at[0])]
    copies[0].start()
    parts = sem.shape[0] - 1
    rows = stack.shape[0] // parts
    for i in range(parts):
        at = pl.ds(i * rows, rows)
        stack[at, :] = jnp.dot(back_op[at, :], back_in[...], preferred_element_type=F32)
        copies.append(pltpu.make_async_copy(stack.at[at], stack_out.at[at], sem.at[i + 1]))
        copies[-1].start()
    for copy in copies:
        copy.wait()


def body(science, template, owners, patch_strip, shifts, fractions, coefs):
    n = lax.axis_size("ccd")
    band, width = science.shape[1:]
    strips, srows = template.shape[3:5]
    capacity = max(2, strips // n)
    slots = n * capacity
    span = capacity * srows
    padded = width + 2 * LANES
    kmain, kedge, kcol = conv_constants(band)
    hbm_spec = pl.BlockSpec(memory_space=pltpu.HBM)
    dma = pltpu.SemaphoreType.DMA
    scratch = [
        pltpu.VMEM((band, width), F32),
        pltpu.VMEM((strips, srows, width), BF16),
        pltpu.SMEM((1, strips), jnp.int32),
        pltpu.SMEM((1, strips), jnp.int32),
        pltpu.SMEM((2, strips), jnp.int32),
        pltpu.SMEM((2, strips), F32),
        pltpu.SMEM((3, 1, 9), F32),
        pltpu.VMEM(kmain.shape, BF16),
        pltpu.VMEM(kedge.shape, BF16),
        pltpu.VMEM(kcol.shape, BF16),
        pltpu.SMEM((n, LANES), jnp.int32),
        pltpu.SMEM((n, LANES), jnp.int32),
        pltpu.SMEM((1, slots), jnp.int32),
        pltpu.VMEM((n, 8, LANES), F32),
        pltpu.VMEM((n, 8, LANES), F32),
        pltpu.VMEM((slots, srows, width), BF16),
        pltpu.VMEM((slots, srows, width), BF16),
        pltpu.VMEM((slots, srows, LANES), BF16),
        pltpu.VMEM((slots, 8, width), F32),
        pltpu.VMEM((slots, 8, width), F32),
        pltpu.VMEM((slots, srows, width), BF16),
        pltpu.VMEM((band, padded), BF16),
        pltpu.VMEM((2, EDGE, padded), BF16),
        pltpu.VMEM((3, band, padded), BF16),
        pltpu.VMEM((width // LANES, 9 * LANES, 2 * LANES), BF16),
        pltpu.VMEM((band, 2 * LANES), F32),
        pltpu.VMEM((strips, srows, width), BF16),
        pltpu.VMEM((2, n * (span - srows // 2), width // 2 + LANES), BF16),
        pltpu.VMEM((n * srows // 2, width), BF16),
        dma((10,)),
        dma((n,)), dma((n,)), dma((n,)), dma((n,)), dma((slots,)), dma((slots,)),
        dma((8,)), dma((8,)),
        dma((3, n)), dma((3, n)),
    ]
    difference, back_in, back_op = pl.pallas_call(
        functools.partial(kernel, capacity=capacity),
        out_shape=(
            jax.ShapeDtypeStruct((band, width), F32),
            jax.ShapeDtypeStruct((n * span, width), BF16),
            jax.ShapeDtypeStruct((band, n * span), BF16),
        ),
        in_specs=[hbm_spec] * 10,
        out_specs=(pl.BlockSpec(memory_space=pltpu.VMEM),) * 3,
        scratch_shapes=scratch,
        compiler_params=pltpu.CompilerParams(
            collective_id=0, has_side_effects=True, vmem_limit_bytes=40 * 1024 * 1024
        ),
    )(
        pltpu.with_memory_space_constraint(science[0], pltpu.HBM),
        pltpu.with_memory_space_constraint(template.reshape(strips, srows, width), pltpu.HBM),
        pltpu.with_memory_space_constraint(owners.reshape(1, strips), pltpu.HBM),
        pltpu.with_memory_space_constraint(patch_strip.reshape(1, strips), pltpu.HBM),
        pltpu.with_memory_space_constraint(shifts.reshape(2, strips), pltpu.HBM),
        pltpu.with_memory_space_constraint(fractions.reshape(2, strips), pltpu.HBM),
        pltpu.with_memory_space_constraint(coefs.transpose(1, 0, 2), pltpu.HBM),
        pltpu.with_memory_space_constraint(jnp.asarray(kmain), pltpu.HBM),
        pltpu.with_memory_space_constraint(jnp.asarray(kedge), pltpu.HBM),
        pltpu.with_memory_space_constraint(jnp.asarray(kcol), pltpu.HBM),
    )
    difference, stack = pl.pallas_call(
        finish,
        out_shape=(
            jax.ShapeDtypeStruct((band, width), F32),
            jax.ShapeDtypeStruct((band, width), F32),
        ),
        in_specs=[pl.BlockSpec(memory_space=pltpu.VMEM)] * 3,
        out_specs=(hbm_spec, hbm_spec),
        scratch_shapes=[pltpu.VMEM((band, width), F32), dma((5,))],
    )(
        pltpu.with_memory_space_constraint(difference, pltpu.VMEM),
        pltpu.with_memory_space_constraint(back_in, pltpu.VMEM),
        pltpu.with_memory_space_constraint(back_op, pltpu.VMEM),
    )
    return difference[None], stack.reshape(template.shape)


def solution(mesh):
    return jax.shard_map(
        body,
        mesh=mesh,
        in_specs=(
            P(("grp", "ccd"), "row", "amp"),
            P(("grp", "ccd"), "row", "amp", None, None, None),
            P(("grp", "ccd"), "row", "amp", None, None),
            P(("grp", "ccd"), "row", "amp", None),
            P(("grp", "ccd"), "row", "amp", None, None),
            P(("grp", "ccd"), "row", "amp", None, None),
            P(("grp", "ccd"), None, None),
        ),
        out_specs=(
            P(("grp", "ccd"), "row", "amp"),
            P(("grp", "ccd"), "row", "amp", None, None, None),
        ),
        check_vma=False,
    )
```

```python
import functools

import jax
import jax.numpy as jnp
import ml_dtypes
import numpy as np
from jax import lax
from jax.experimental import pallas as pl
from jax.experimental.pallas import tpu as pltpu
from jax.sharding import PartitionSpec as P

RADIUS = 9
EDGE = 16
LANES = 128
TILE = 256
MESH = pl.DeviceIdType.MESH
F32 = jnp.float32
BF16 = jnp.bfloat16


def kernel_table():
    support = np.arange(-RADIUS, RADIUS + 1).astype(np.float32)
    narrow = np.exp(-support * support / np.float32(4.5))
    slope = support * np.exp(-support * support / np.float32(12.5))
    broad = np.exp(-support * support / np.float32(40.5))
    table = np.stack(
        [narrow / np.sum(narrow), slope / np.sum(np.abs(slope)), broad / np.sum(broad)]
    )
    return table.astype(ml_dtypes.bfloat16)


def toeplitz(kernel, out_at, in_at):
    offset = in_at[None, :] - out_at[:, None] + RADIUS
    inside = (offset >= 0) & (offset <= 2 * RADIUS)
    return np.where(inside, kernel[np.clip(offset, 0, 2 * RADIUS)], np.zeros((), kernel.dtype))


def conv_constants(rows):
    table = kernel_table()
    at = np.arange(rows)
    main = np.concatenate([toeplitz(k, at, at) for k in table], axis=0)
    top = np.stack([toeplitz(k, np.arange(EDGE), np.arange(-EDGE, 0)) for k in table])
    bottom = np.stack(
        [toeplitz(k, np.arange(-EDGE, 0), np.arange(EDGE)) for k in table]
    )
    source = np.arange(-EDGE, LANES + EDGE)
    cols = np.stack([toeplitz(k, np.arange(LANES), source).T for k in table])
    return main, np.stack([top, bottom]), cols


def sinc(value):
    angle = np.float32(np.pi) * value
    return jnp.sin(angle) / angle


def taps_of(offset):
    value = sinc(offset) * sinc(offset / 3.0)
    return value.astype(BF16).astype(F32)


def kernel(
    sci_hbm, tmpl_hbm, own_hbm, pat_hbm, shf_hbm, frc_hbm, cof_hbm, kmain_hbm, kedge_hbm, kcol_hbm,
    diff, back_in, back_op,
    sci, tmpl, own, pat, shf, frc, cof, kmain, kedge, kcol,
    req_out, req_in, strip_at, meta_out, meta_in, send_buf, fetch, warp_op, taps_fwd, taps_bwd, slot_img,
    img, halo_rows, across, col_op, acc, low, back_free, back_late,
    load_sem, req_send, req_recv, meta_send, meta_recv, tmpl_send, tmpl_recv,
    halo_send, halo_recv, back_send, back_recv,
    *, capacity,
):
    n = lax.axis_size("ccd")
    rows_n = lax.axis_size("row")
    cols_n = lax.axis_size("amp")
    me = lax.axis_index("ccd")
    my_row = lax.axis_index("row")
    my_col = lax.axis_index("amp")
    strips, srows, width = tmpl.shape
    band = strips * srows
    span = capacity * srows
    slots = n * capacity
    padded = width + 2 * LANES

    if n == 4:
        low_half = me < n // 2
        at_end = (me == 0) | (me == n - 1)
        near = [jnp.where(low_half, 3, 1), jnp.where(at_end, 2, jnp.where(low_half, 1, 3))]
        near.append(6 - near[0] - near[1])
        distant = [jnp.where(me == 0, 3, jnp.where(me == n - 1, 1, 2)), jnp.where(at_end, 2, jnp.where(low_half, 1, 3))]
        distant.append(6 - distant[0] - distant[1])
    else:
        near = distant = list(range(1, n))

    def peer(d):
        return {"ccd": lax.rem(me + d, n)}

    def back_peer(d):
        return {"ccd": lax.rem(me + n - d, n)}

    other_row = 1 - 2 * my_row
    other_col = 1 - 2 * my_col
    if rows_n == 2:
        steps = [(0, other_col), (other_row, 0), (other_row, other_col)]
    else:
        steps = [(-1, 0), (1, 0), (0, other_col), (-1, other_col), (1, other_col)]

    def when(step):
        if rows_n == 2 or (not isinstance(step[0], int)) or step[0] == 0:
            return lambda run: run()
        return pl.when((my_row + step[0] >= 0) & (my_row + step[0] < rows_n))

    def neighbour(step):
        return {"row": my_row + step[0], "amp": my_col + step[1]}

    barrier = pltpu.get_barrier_semaphore()
    for d in range(1, n):
        pl.semaphore_signal(barrier, inc=1, device_id=peer(d), device_id_type=MESH)
    for step in steps:
        @when(step)
        def _():
            pl.semaphore_signal(barrier, inc=1, device_id=neighbour(step), device_id_type=MESH)

    loads = [
        pltpu.make_async_copy(src, dst, load_sem.at[i])
        for i, (src, dst) in enumerate(
            [(own_hbm, own), (pat_hbm, pat), (shf_hbm, shf), (frc_hbm, frc), (cof_hbm, cof),
             (tmpl_hbm, tmpl), (kmain_hbm, kmain), (kedge_hbm, kedge), (kcol_hbm, kcol), (sci_hbm, sci)]
        )
    ]
    for load in loads:
        load.start()

    loads[0].wait()
    loads[1].wait()
    owner = [own[0, q] for q in range(strips)]
    slot_of = []
    for q in range(strips):
        rank = jnp.int32(0)
        for e in range(q):
            alike = owner[e] == owner[q]
            rank = rank + jnp.where(alike & (my_row == 0) if e == 0 else alike, 1, 0)
        if q == 0:
            rank = jnp.where(my_row == 0, rank, capacity - 1)
        if q == strips - 1:
            rank = jnp.where(my_row == 0, capacity - 1, rank)
        away = owner[q] - me
        away = jnp.where(away < 0, away + n, away)
        slot_of.append(jnp.minimum(away * capacity + rank, slots - 1))
    strip_of = []
    wanted = []
    for s in range(slots):
        q_at = jnp.int32(-1)
        for q in range(strips):
            q_at = jnp.where(slot_of[q] == s, q, q_at)
        q_in = jnp.maximum(q_at, 0)
        strip_of.append(q_in)
        strip_at[0, s] = q_in
        wanted.append(jnp.where(q_at < 0, -1, pat[0, q_in]))
    for d in range(1, n):
        for r in range(capacity):
            req_out[d, r] = jnp.maximum(wanted[d * capacity + r], 0)

    if rows_n == 2:
        around = n - 1 + len(steps)
    else:
        ends = jnp.where(my_row == 0, 1, 0) + jnp.where(my_row == rows_n - 1, 1, 0)
        around = n - 1 + len(steps) - 2 * ends
    pl.semaphore_wait(barrier, around)

    def request(d):
        return pltpu.make_async_remote_copy(
            src_ref=req_out.at[d], dst_ref=req_in.at[d], send_sem=req_send.at[d], recv_sem=req_recv.at[d],
            device_id=peer(d), device_id_type=MESH)

    for d in range(1, n):
        request(d).start()

    loads[5].wait()
    for r in range(capacity):
        fetch[r] = tmpl[jnp.maximum(wanted[r], 0)]

    def reply(d, r):
        s = d * capacity + r
        return pltpu.make_async_remote_copy(
            src_ref=send_buf.at[s], dst_ref=fetch.at[s], send_sem=tmpl_send.at[s], recv_sem=tmpl_recv.at[s],
            device_id=back_peer(d), device_id_type=MESH)

    for d in near:
        request(d).wait_recv()
        for r in range(capacity):
            send_buf[d * capacity + r] = tmpl[req_in[d, r]]
        reply(d, 0).start()
    for r in range(1, capacity):
        for d in near:
            reply(d, r).start()

    lane = lax.broadcasted_iota(jnp.int32, (8, LANES), 1)
    sub = lax.broadcasted_iota(jnp.int32, (8, LANES), 0)
    tap = (sub - 2).astype(F32)

    def meta(d):
        return pltpu.make_async_remote_copy(
            src_ref=meta_out.at[d], dst_ref=meta_in.at[d], send_sem=meta_send.at[d], recv_sem=meta_recv.at[d],
            device_id=peer(d), device_id_type=MESH)

    for i in range(2, 4):
        loads[i].wait()

    def slot_table(s):
        taps = taps_of(tap - frc[0, strip_of[s]])
        return taps, shf[0, strip_of[s]]

    def meta_table(d, rank):
        frac = jnp.full((8, LANES), 0.5, F32)
        shift = jnp.zeros((8, LANES), F32)
        which = jnp.full((8, LANES), -1.0, F32)
        for r in range(capacity):
            s = d * capacity + r
            frac = jnp.where(rank == r, frc[0, strip_of[s]], frac)
            shift = jnp.where(rank == r, shf[0, strip_of[s]].astype(F32), shift)
            which = jnp.where(rank == r, wanted[s].astype(F32), which)
        taps = taps_of(tap - frac)
        return jnp.where(sub == 6, shift, jnp.where(sub == 7, which, taps))

    part_rows = srows // 2
    for d in list(range(1, n)) + [0]:
        meta_out[d] = meta_table(d, lax.rem(lane // srows, capacity))
        if d:
            meta(d).start()

    row_at = lax.broadcasted_iota(jnp.int32, (srows, LANES), 0)
    lane_at = lax.broadcasted_iota(jnp.int32, (srows, LANES), 1)

    def place(table, offset):
        total = jnp.zeros((srows, LANES), F32)
        for t in range(6):
            total = jnp.where(offset == t - 2, table[t:t + 1, :], total)
        return total

    for s in range(slots):
        taps, shift = slot_table(s)
        warp_op[s] = place(taps, lane_at - row_at - shift).astype(BF16)

    col_at = lax.broadcasted_iota(jnp.int32, (8, width), 1)
    tap_at = lax.broadcasted_iota(jnp.int32, (8, width), 0) - 2
    for s in range(slots):
        taps = taps_of(tap - frc[1, strip_of[s]])
        wide = jnp.concatenate([taps] * (width // LANES), axis=1)
        moved = tap_at + shf[1, strip_of[s]]
        ahead, behind = col_at + moved, col_at - moved
        taps_fwd[s] = jnp.where((ahead >= 0) & (ahead < width), wide, 0.0)
        taps_bwd[s] = jnp.where((behind >= 0) & (behind < width), wide, 0.0)

    for i in (4, 6, 7, 8):
        loads[i].wait()
    tiles = width // LANES
    window = 3 * LANES
    first = LANES - EDGE
    last = 2 * LANES + EDGE
    place_x = lax.broadcasted_iota(jnp.int32, (1, LANES), 1).astype(F32) + (my_col * width).astype(F32)
    for j in range(tiles):
        for a in range(3):
            col_op[j, a * window:a * window + first, :] = jnp.zeros((first, 2 * LANES), BF16)
            col_op[j, a * window + last:(a + 1) * window, :] = jnp.zeros((window - last, 2 * LANES), BF16)
    chunk = 80
    for a in range(3):
        @pl.loop(0, (last - first) // chunk)
        def _(i):
            at = pl.ds(pl.multiple_of(i * chunk, 16), chunk)
            base = [kcol[b, at, :].astype(F32) for b in range(3)]
            fold = [
                cof[j, 0, 3 * a] * base[0] + cof[j, 0, 3 * a + 1] * base[1] + cof[j, 0, 3 * a + 2] * base[2]
                for j in range(3)
            ]
            to = pl.ds(pl.multiple_of(a * window + first + i * chunk, 16), chunk)
            for j in range(tiles):
                px = (place_x + (j * LANES + 0.5)) / (width * cols_n) * 2.0 - 1.0
                col_op[j, to, 0:LANES] = (fold[0] + px * fold[1]).astype(BF16)
                col_op[j, to, LANES:] = fold[2].astype(BF16)

    if rows_n == 2:
        halves_at = [pl.multiple_of(part_rows * my_row, part_rows), pl.multiple_of(part_rows * (1 - my_row), part_rows)]
    else:
        halves_at = [0, part_rows]
    late = part_rows
    free = span - late
    group = LANES // span

    right = LANES + width
    col_in = pl.multiple_of(jnp.where(my_col == 0, right, 0), LANES)
    col_out = pl.multiple_of(jnp.where(my_col == 0, 0, right), LANES)
    img[:, pl.ds(col_out, LANES)] = jnp.zeros((band, LANES), BF16)
    halo_rows[:, :, pl.ds(col_out, LANES)] = jnp.zeros((2, EDGE, LANES), BF16)
    if rows_n > 2:
        @pl.when(my_row == 0)
        def _():
            halo_rows[0] = jnp.zeros((EDGE, padded), BF16)

        @pl.when(my_row == rows_n - 1)
        def _():
            halo_rows[1] = jnp.zeros((EDGE, padded), BF16)
    for a in range(3):
        across[a, :, pl.ds(col_out, LANES)] = jnp.zeros((band, LANES), BF16)

    for r in range(capacity):
        for d in range(n):
            s = d * capacity + r
            if d:
                reply(d, r).wait_recv()
            value = jnp.dot(warp_op[s, :, :srows], fetch[s], preferred_element_type=F32).astype(BF16)
            move = shf[1, strip_of[s]]
            total = jnp.zeros((srows, width), F32)
            for t in range(6):
                moved = pltpu.roll(value, width - (move + (t - 2)), 1).astype(F32)
                total = total + taps_fwd[s, t:t + 1, :] * moved
            slot_img[s] = total.astype(BF16)
    for q in range(strips):
        img[q * srows:(q + 1) * srows, LANES:right] = slot_img[slot_of[q]]

    def halo(i):
        step = steps[i]
        if isinstance(step[1], int):
            cols_src = cols_dst = pl.ds(LANES, width)
        else:
            cols_src = pl.ds(pl.multiple_of(jnp.where(my_col == 0, right - LANES, LANES), LANES), LANES)
            cols_dst = pl.ds(col_out, LANES)
        if isinstance(step[0], int) and step[0] == 0:
            src, dst = img.at[:, cols_src], img.at[:, cols_dst]
        elif isinstance(step[0], int):
            top = band - EDGE if step[0] > 0 else 0
            src = img.at[pl.ds(top, EDGE), cols_src]
            dst = halo_rows.at[0 if step[0] > 0 else 1, :, cols_dst]
        else:
            top = pl.multiple_of(jnp.where(my_row == 0, band - EDGE, 0), EDGE)
            src = img.at[pl.ds(top, EDGE), cols_src]
            dst = halo_rows.at[my_row, :, cols_dst]
        return pltpu.make_async_remote_copy(
            src_ref=src, dst_ref=dst, send_sem=halo_send.at[i], recv_sem=halo_recv.at[i],
            device_id=neighbour(step), device_id_type=MESH)

    for i, step in enumerate(steps):
        @when(step)
        def _(i=i):
            halo(i).start()

    def received(step):
        if isinstance(step[0], int):
            return (-step[0], step[1])
        return step

    def await_halo(at):
        @when(received(steps[at]))
        def _():
            halo(at).wait_recv()

    def across_of(col, count):
        for a in range(3):
            total = jnp.dot(kmain[a * band:(a + 1) * band, :], img[:, pl.ds(col, count)], preferred_element_type=F32)
            across[a, :, pl.ds(col, count)] = total.astype(BF16)

    if rows_n == 2:
        edges = [(1 - my_row, pl.multiple_of(jnp.where(my_row == 0, band - EDGE, 0), EDGE))]
    else:
        edges = [(0, 0), (1, band - EDGE)]

    def edge_rows():
        for a in range(3):
            for side, top in edges:
                near = kmain[pl.ds(pl.multiple_of(a * band + top, EDGE), EDGE), :]
                total = jnp.dot(near, img[...], preferred_element_type=F32)
                total = total + jnp.dot(kedge[side, a], halo_rows[side], preferred_element_type=F32)
                across[a, pl.ds(top, EDGE), :] = total.astype(BF16)

    def subtract(turn, top, rows):
        tile = my_col * (tiles - 1) + turn * (1 - 2 * my_col)
        here = pl.ds(top, rows)
        at = pl.ds(pl.multiple_of(tile * LANES, LANES), window)
        lhs = jnp.concatenate([across[a, here, at] for a in range(3)], axis=1)
        model = jnp.dot(lhs, col_op[tile], preferred_element_type=F32)
        at = pl.ds(pl.multiple_of(tile * LANES, LANES), LANES)
        step = min(rows, srows)
        local = lax.broadcasted_iota(jnp.int32, (step, LANES), 0)
        for q in range(rows // step):
            y = local + (my_row * band + top + q * step)
            py = (y.astype(F32) + 0.5) / (band * rows_n) * 2.0 - 1.0
            part = slice(q * step, (q + 1) * step)
            to = pl.ds(pl.multiple_of(top + q * step, step), step)
            value = sci[to, at] - (model[part, 0:LANES] + py * model[part, LANES:])
            diff[to, at] = value
            strip = top // srows + q
            low[strip, pl.ds(pl.multiple_of(top - top // srows * srows, step), step), at] = value.astype(BF16)

    piece_cols = width // 2
    region = piece_cols + LANES

    def piece_at(piece):
        inner = my_col if piece == 0 else 1 - my_col
        return pl.multiple_of(inner * piece_cols, LANES), pl.multiple_of(inner * LANES, LANES)

    def give(d, piece):
        if piece == 2:
            src = back_late.at[pl.ds(pl.multiple_of(d * late, late), late)]
            dst = back_in.at[pl.ds(pl.multiple_of(d * span + free, late), late)]
        else:
            at, offset = piece_at(piece)
            src = back_free.at[piece, pl.ds(pl.multiple_of(d * free, late), free), pl.ds(offset, piece_cols)]
            dst = back_in.at[pl.ds(pl.multiple_of(d * span, late), free), pl.ds(at, piece_cols)]
        return pltpu.make_async_remote_copy(
            src_ref=src, dst_ref=dst, send_sem=back_send.at[piece, d], recv_sem=back_recv.at[piece, d],
            device_id=peer(d), device_id_type=MESH)

    def column_sum(s, top, rows, source, cols):
        value = low[strip_at[0, s], pl.ds(top, rows), source]
        move = shf[1, strip_at[0, s]]
        total = jnp.zeros((rows, cols), F32)
        for t in range(6):
            moved = pltpu.roll(value, cols + (move + (t - 2)), 1).astype(F32)
            total = total + taps_bwd[s, t:t + 1, source] * moved
        return total.astype(BF16)

    def columns_back(piece):
        if piece < 2:
            at, offset = piece_at(piece)
            source = pl.ds(pl.multiple_of(at - offset, LANES), region)
        for d in distant:
            if piece == 2:
                back_late[pl.ds(pl.multiple_of(d * late, late), late), :] = column_sum(
                    (d + 1) * capacity - 1, halves_at[1], late, pl.ds(0, width), width)
            else:
                for r in range(capacity):
                    rows = srows if r < capacity - 1 else srows - late
                    top = 0 if r < capacity - 1 else halves_at[0]
                    to = pl.ds(pl.multiple_of(d * free + r * srows, late), rows)
                    back_free[piece, to, :] = column_sum(d * capacity + r, top, rows, source, region)
            give(d, piece).start()

    amp_at = [i for i, step in enumerate(steps) if isinstance(step[0], int) and step[0] == 0]
    row_at_steps = [i for i in range(len(steps)) if i not in amp_at]

    def finish_edges():
        for i in row_at_steps:
            await_halo(i)
        edge_rows()

    loads[9].wait()
    for c in range(width // TILE):
        across_of(pl.multiple_of(LANES + (c + (1 - 2 * c) * my_col) * TILE, LANES), TILE)
    if rows_n > 2:
        for i in amp_at:
            await_halo(i)
        across_of(col_in, LANES)
        finish_edges()
    for turn in range(tiles - 1):
        subtract(turn, 0, band // 2)
        subtract(turn, band // 2, band // 2)
    columns_back(0)
    if rows_n == 2:
        for i in amp_at:
            await_halo(i)
        across_of(col_in, LANES)
    subtract(tiles - 1, 0, band)
    columns_back(1)
    if rows_n == 2:
        finish_edges()
        for turn in range(tiles):
            subtract(turn, edges[0][1], EDGE)
    columns_back(2)

    everywhere = pl.ds(0, width)
    for r in range(capacity - 1):
        back_in[r * srows:(r + 1) * srows, :] = column_sum(r, 0, srows, everywhere, width)
    back_in[span - srows:free, :] = column_sum(capacity - 1, halves_at[0], srows - late, everywhere, width)
    back_in[free:span, :] = column_sum(capacity - 1, halves_at[1], late, everywhere, width)

    span_at = lax.rem(lane_at, span)
    late_at = lax.rem(span_at, part_rows) + jnp.where(span_at < free, halves_at[0], halves_at[1])
    from_row = jnp.where(span_at < span - srows, lax.rem(span_at, srows), late_at)
    for g in range(n // group):
        for e in range(group):
            d = g * group + e
            if d:
                meta(d).wait_recv()
            came = meta_in[d] if d else meta_out[0]
            table = came if e == 0 else jnp.where(lane // span == e, came, table)
        shift = table[6:7, :].astype(jnp.int32)
        which = table[7:8, :].astype(jnp.int32)
        operator = place(table, row_at - from_row - shift)
        for p in range(strips):
            back_op[p * srows:(p + 1) * srows, g * LANES:(g + 1) * LANES] = jnp.where(which == p, operator, 0.0).astype(BF16)

    for piece in range(3):
        for d in range(1, n):
            give(d, piece).wait_recv()

    for d in range(1, n):
        request(d).wait_send()
        for r in range(capacity):
            reply(d, r).wait_send()
        meta(d).wait_send()
        for piece in range(3):
            give(d, piece).wait_send()
    for i, step in enumerate(steps):
        @when(step)
        def _(i=i):
            halo(i).wait_send()


def finish(diff, back_in, back_op, diff_out, stack_out, stack, sem):
    copies = [pltpu.make_async_copy(diff, diff_out, sem.at[0])]
    copies[0].start()
    parts = sem.shape[0] - 1
    rows = stack.shape[0] // parts
    for i in range(parts):
        at = pl.ds(i * rows, rows)
        stack[at, :] = jnp.dot(back_op[at, :], back_in[...], preferred_element_type=F32)
        copies.append(pltpu.make_async_copy(stack.at[at], stack_out.at[at], sem.at[i + 1]))
        copies[-1].start()
    for copy in copies:
        copy.wait()


def body(science, template, owners, patch_strip, shifts, fractions, coefs):
    n = lax.axis_size("ccd")
    band, width = science.shape[1:]
    strips, srows = template.shape[3:5]
    capacity = max(2, strips // n)
    slots = n * capacity
    span = capacity * srows
    padded = width + 2 * LANES
    kmain, kedge, kcol = conv_constants(band)
    hbm_spec = pl.BlockSpec(memory_space=pltpu.HBM)
    dma = pltpu.SemaphoreType.DMA
    scratch = [
        pltpu.VMEM((band, width), F32),
        pltpu.VMEM((strips, srows, width), BF16),
        pltpu.SMEM((1, strips), jnp.int32),
        pltpu.SMEM((1, strips), jnp.int32),
        pltpu.SMEM((2, strips), jnp.int32),
        pltpu.SMEM((2, strips), F32),
        pltpu.SMEM((3, 1, 9), F32),
        pltpu.VMEM(kmain.shape, BF16),
        pltpu.VMEM(kedge.shape, BF16),
        pltpu.VMEM(kcol.shape, BF16),
        pltpu.SMEM((n, LANES), jnp.int32),
        pltpu.SMEM((n, LANES), jnp.int32),
        pltpu.SMEM((1, slots), jnp.int32),
        pltpu.VMEM((n, 8, LANES), F32),
        pltpu.VMEM((n, 8, LANES), F32),
        pltpu.VMEM((slots, srows, width), BF16),
        pltpu.VMEM((slots, srows, width), BF16),
        pltpu.VMEM((slots, srows, LANES), BF16),
        pltpu.VMEM((slots, 8, width), F32),
        pltpu.VMEM((slots, 8, width), F32),
        pltpu.VMEM((slots, srows, width), BF16),
        pltpu.VMEM((band, padded), BF16),
        pltpu.VMEM((2, EDGE, padded), BF16),
        pltpu.VMEM((3, band, padded), BF16),
        pltpu.VMEM((width // LANES, 9 * LANES, 2 * LANES), BF16),
        pltpu.VMEM((band, 2 * LANES), F32),
        pltpu.VMEM((strips, srows, width), BF16),
        pltpu.VMEM((2, n * (span - srows // 2), width // 2 + LANES), BF16),
        pltpu.VMEM((n * srows // 2, width), BF16),
        dma((10,)),
        dma((n,)), dma((n,)), dma((n,)), dma((n,)), dma((slots,)), dma((slots,)),
        dma((8,)), dma((8,)),
        dma((3, n)), dma((3, n)),
    ]
    difference, back_in, back_op = pl.pallas_call(
        functools.partial(kernel, capacity=capacity),
        out_shape=(
            jax.ShapeDtypeStruct((band, width), F32),
            jax.ShapeDtypeStruct((n * span, width), BF16),
            jax.ShapeDtypeStruct((band, n * span), BF16),
        ),
        in_specs=[hbm_spec] * 10,
        out_specs=(pl.BlockSpec(memory_space=pltpu.VMEM),) * 3,
        scratch_shapes=scratch,
        compiler_params=pltpu.CompilerParams(
            collective_id=0, has_side_effects=True, vmem_limit_bytes=40 * 1024 * 1024
        ),
    )(
        pltpu.with_memory_space_constraint(science[0], pltpu.HBM),
        pltpu.with_memory_space_constraint(template.reshape(strips, srows, width), pltpu.HBM),
        pltpu.with_memory_space_constraint(owners.reshape(1, strips), pltpu.HBM),
        pltpu.with_memory_space_constraint(patch_strip.reshape(1, strips), pltpu.HBM),
        pltpu.with_memory_space_constraint(shifts.reshape(2, strips), pltpu.HBM),
        pltpu.with_memory_space_constraint(fractions.reshape(2, strips), pltpu.HBM),
        pltpu.with_memory_space_constraint(coefs.transpose(1, 0, 2), pltpu.HBM),
        pltpu.with_memory_space_constraint(jnp.asarray(kmain), pltpu.HBM),
        pltpu.with_memory_space_constraint(jnp.asarray(kedge), pltpu.HBM),
        pltpu.with_memory_space_constraint(jnp.asarray(kcol), pltpu.HBM),
    )
    difference, stack = pl.pallas_call(
        finish,
        out_shape=(
            jax.ShapeDtypeStruct((band, width), F32),
            jax.ShapeDtypeStruct((band, width), F32),
        ),
        in_specs=[pl.BlockSpec(memory_space=pltpu.VMEM)] * 3,
        out_specs=(hbm_spec, hbm_spec),
        scratch_shapes=[pltpu.VMEM((band, width), F32), dma((5,))],
    )(
        pltpu.with_memory_space_constraint(difference, pltpu.VMEM),
        pltpu.with_memory_space_constraint(back_in, pltpu.VMEM),
        pltpu.with_memory_space_constraint(back_op, pltpu.VMEM),
    )
    return difference[None], stack.reshape(template.shape)


def solution(mesh):
    return jax.shard_map(
        body,
        mesh=mesh,
        in_specs=(
            P(("grp", "ccd"), "row", "amp"),
            P(("grp", "ccd"), "row", "amp", None, None, None),
            P(("grp", "ccd"), "row", "amp", None, None),
            P(("grp", "ccd"), "row", "amp", None),
            P(("grp", "ccd"), "row", "amp", None, None),
            P(("grp", "ccd"), "row", "amp", None, None),
            P(("grp", "ccd"), None, None),
        ),
        out_specs=(
            P(("grp", "ccd"), "row", "amp"),
            P(("grp", "ccd"), "row", "amp", None, None, None),
        ),
        check_vma=False,
    )
```
